32 devices in a mesh: dp: 8 (over y, x, core), mp: 4 (over z).
Axes of the slice: x: 2, y: 2, z: 4, core: 2. Of those that a mesh axis runs over, the one named last changes fastest.
Arguments:
- tokens: bfloat16 [2048, 4096], P('dp'), may hold values from -6 to 6
- pack_source: int32 [2048], P('dp'), may hold values from 0 to 2047, as said below
- segment_ids: int32 [2048], P('dp'), may hold values from 0 to 3, never falling along the last dimension, each value on 1 to 1536 neighbouring positions
- w_in: bfloat16 [4096, 20480], P('dp', 'mp'), may hold values from -0.09375 to 0.09375
- w_dt: bfloat16 [4096, 128], P('dp', 'mp'), may hold values from -0.09375 to 0.09375
- w_out: bfloat16 [4096, 8192], P(None, 'mp'), may hold values from -0.0625 to 0.0625
- conv_x: float32 [4, 8192], P(None, 'mp'), may hold values from -3 to 3
- conv_bc: float32 [4, 2, 2048], P(None, None, 'mp'), may hold values from -3 to 3
- dt_bias: float32 [128], P('mp'), may hold values from -5 to -3
- decay_rate: float32 [128], P('mp'), may hold values from 0.0625 to 0.5
- skip_gain: float32 [128], P('mp'), may hold values from 0.1 to 0.5
- norm_gain: float32 [8192], P('mp'), may hold values from 0.1 to 1.9
Outputs:
- mixed: bfloat16 [2048, 4096], P(('dp', 'mp'))
The draws below stay inside these ranges and needn't reach their ends.
Inputs may be any that keep to these rules, and one draw needn't show every extreme that they name: pack_source is a permutation of the generation-order rows. Taking aligned blocks of 256 rows on both sides, a block of packed positions holds at most 64 rows of any one block of generation-order rows; each packed block holds exactly 64 rows of exactly one generation block, and each generation block gives exactly 64 rows to exactly one packed block. `segment_ids`: non-decreasing; each response has 1 to 1536 positions and one has exactly 1536.
All inputs are finite; a program needn't handle non-finite values.
Results may differ from the reference program's by a relative error of at most 0.012.
Values may be sent and summed in bfloat16 or wider, within the bound.
A program may use at most 192 MiB of HBM per device.

```python
import math
import jax
import jax.numpy as jnp
import numpy as np
from jax import lax

D = 4096
HEADS = 128
HEAD_DIM = 64
GROUPS = 8
STATE = 256
CONV = 4
BLOCK = 256
TOK_DEV = 256
DI = 8192
GN = 2048
PANEL = 5120
CAP = 64
TOKENS = 2048
SEGS = 4
SEG_MOST = 1536
N_DP = 8
N_MP = 4


def draw_pack_source(key, part):
    key_list = jax.random.split(jax.random.fold_in(key, 11), 6)
    device_count = N_DP
    row_total = TOK_DEV
    capacity = CAP
    lane_ids = jnp.arange(device_count, dtype=jnp.int32)
    peak_lane = jax.random.randint(key_list[0], (), 0, device_count)
    weights = jax.random.randint(key_list[1], (device_count,), 2, 4)
    weights = jnp.where(lane_ids == peak_lane, 0, weights).astype(jnp.int32)
    cum_weight = jnp.cumsum(weights).astype(jnp.int32)
    spread = (row_total - capacity) * cum_weight // cum_weight[-1]
    base_counts = spread - jnp.concatenate([jnp.zeros((1,), jnp.int32), spread[:-1]])
    base_counts = base_counts + capacity * (lane_ids == peak_lane).astype(jnp.int32)
    perm_source = jax.random.permutation(key_list[2], device_count)
    perm_target = jax.random.permutation(key_list[3], device_count)
    counts = base_counts[(perm_source[:, None] + perm_target[None, :]) % device_count]
    end_source = jnp.cumsum(counts, axis=1)
    start_source = end_source - counts
    start_target = jnp.cumsum(counts, axis=0) - counts
    positions = jnp.arange(row_total, dtype=jnp.int32)
    owner_dev = jnp.sum((positions[None, :, None] >= end_source[:, None, :]).astype(jnp.int32), axis=2)
    within = positions[None, :] - jnp.take_along_axis(start_source, owner_dev, axis=1)
    place_pre = jnp.take_along_axis(start_target, owner_dev, axis=1) + within
    source_perm = jax.vmap(lambda sub_key: jax.random.permutation(sub_key, row_total))(jax.random.split(key_list[4], device_count))
    target_perm = jax.vmap(lambda sub_key: jax.random.permutation(sub_key, row_total))(jax.random.split(key_list[5], device_count))
    slot_final = target_perm[owner_dev, place_pre]
    source_rows = lane_ids[:, None] * row_total + source_perm
    target_rows = owner_dev * row_total + slot_final
    packing = jnp.zeros((device_count * row_total,), jnp.int32).at[target_rows.reshape(-1)].set(source_rows.reshape(-1).astype(jnp.int32))
    return packing


def block_levels(own_key, extent, cuts, low, top_value):
    loudness, own = 1.0, jax.random.fold_in(own_key, 6)
    for axis_at, parts in cuts:
        steps = jnp.exp(jax.random.uniform(jax.random.fold_in(own, axis_at), (parts,), jnp.float32, low / len(cuts), top_value / len(cuts)))
        loudness = loudness * jnp.repeat(steps, extent[axis_at] // parts).reshape([-1 if axis == axis_at else 1 for axis in range(len(extent))])
    return loudness


def profile(amount, total, reach, skew):
    portions = [(1 << 20) // math.isqrt(grade ** skew) + 1 for grade in range(2, amount + 1)]
    rest, holding = total - reach - (amount - 1), [1] * (amount - 1)
    while rest > 0:
        free = [i for i in range(amount - 1) if holding[i] < reach]
        mass, remaining = sum([portions[i] for i in free]), rest
        for i in free:
            more = min(reach - holding[i], max(1, remaining * portions[i] // mass), rest)
            holding[i] = holding[i] + more
            rest = rest - more
    return np.array([reach] + holding)


def ragged(rng, number_of, total, reach, lean):
    if number_of == 2:
        one = jax.random.randint(rng, (), max(1, total - reach), min(reach, total - 1) + 1)
        return jnp.stack([one, total - one])
    sizes = jnp.asarray(profile(number_of, total, reach, lean), jnp.int32)
    couples = (number_of - 1) // 2
    donor, receiver = sizes[1:1 + 2 * couples:2], sizes[2:2 + 2 * couples:2]
    room = jnp.minimum(donor - 1, reach - receiver)
    moved = jax.random.randint(jax.random.fold_in(rng, 1), (couples,), 0, 1 << 20) % (room + 1)
    sizes = sizes.at[1:1 + 2 * couples:2].set(donor - moved).at[2:2 + 2 * couples:2].set(receiver + moved)
    return sizes[jax.random.permutation(jax.random.fold_in(rng, 2), number_of)]


def gaussian(rng, extent, scale, limit, cuts=(), kind=jnp.bfloat16):
    result = jax.random.normal(rng, extent, jnp.float32) * scale
    if len(cuts) > 0:
        result = block_levels(rng, extent, cuts, -0.22, 0.18) * result
    return jnp.clip(result, min=-limit, max=limit).astype(kind)


def setup_inputs(seed: int = 0) -> dict:
    streams_of = jax.random.split(jax.random.key(seed), 13)
    tokens = gaussian(streams_of[0], (TOKENS, D), 1.0, 6.0, ((0, 8),))
    pack_source = draw_pack_source(jax.random.fold_in(streams_of[12], 71), 0)
    segment_ids = jnp.searchsorted(jnp.cumsum(ragged(streams_of[2], SEGS, TOKENS, SEG_MOST, 1)), jnp.arange(TOKENS), side="right").astype(jnp.int32)
    w_in = gaussian(streams_of[3], (D, 2 * DI + 2 * GN), D ** -0.5, 0.09375, ((0, 8), (1, 4)))
    w_dt = gaussian(streams_of[4], (D, HEADS), D ** -0.5, 0.09375, ((0, 8), (1, 4)))
    w_out = gaussian(streams_of[5], (D, DI), DI ** -0.5, 0.0625, ((1, 4),))
    conv_x = gaussian(streams_of[6], (CONV, DI), 0.5, 3.0, ((1, 4),), jnp.float32)
    conv_bc = gaussian(streams_of[7], (CONV, 2, GN), 0.5, 3.0, ((2, 4),), jnp.float32)
    dt_bias = jnp.clip(-5.0 + 2.0 * jax.random.uniform(streams_of[8], (HEADS,), jnp.float32) ** block_levels(streams_of[8], (HEADS,), ((0, 4),), -0.2, 0.2), -5.0, -3.0)
    decay_rate = jnp.clip(jnp.exp(math.log(0.5) - 2.0794415 * jax.random.uniform(streams_of[9], (HEADS,), jnp.float32) ** block_levels(streams_of[9], (HEADS,), ((0, 4),), -0.2, 0.2)), 0.0625, 0.5)
    skip_gain = jnp.clip(0.1 + 0.4 * jax.random.uniform(streams_of[10], (HEADS,), jnp.float32) ** block_levels(streams_of[10], (HEADS,), ((0, 4),), -0.2, 0.2), 0.1, 0.5)
    norm_gain = jnp.clip(1.0 + 0.18 * jax.random.normal(streams_of[11], (DI,), jnp.float32), 0.1, 1.9)
    return dict(tokens=tokens, pack_source=pack_source, segment_ids=segment_ids, w_in=w_in, w_dt=w_dt, w_out=w_out, conv_x=conv_x, conv_bc=conv_bc, dt_bias=dt_bias, decay_rate=decay_rate, skip_gain=skip_gain, norm_gain=norm_gain)


highest = lax.Precision.HIGHEST

def block_step(carry, pieces):
    state_now, prev_seg = carry
    x_block, b_block, c_block, step_dt, step_rate, seg_block = pieces
    per_group = x_block.shape[1] // b_block.shape[1]
    cum_rate = jnp.cumsum(step_rate, axis=0)
    places = jnp.arange(seg_block.shape[0])
    linked = (seg_block[:, None] == seg_block[None, :]) & (places[:, None] >= places[None, :])
    log_spans = cum_rate.T[:, :, None] - cum_rate.T[:, None, :]
    decay_mat = jnp.where(linked[None], jnp.exp(jnp.where(linked[None], log_spans, 0.0)), 0.0)
    scores = jnp.einsum('tgn,sgn->gts', c_block.astype(jnp.float32), b_block.astype(jnp.float32), precision=highest)
    scores = jnp.repeat(scores, per_group, axis=0)
    mixing = (scores * decay_mat * step_dt.T[:, None, :]).astype(jnp.bfloat16)
    in_block = jnp.einsum('hts,shp->thp', mixing.astype(jnp.float32), x_block.astype(jnp.float32), precision=highest)
    c_heads = jnp.repeat(c_block.astype(jnp.float32), per_group, axis=1)
    b_heads = jnp.repeat(b_block.astype(jnp.float32), per_group, axis=1)
    entry_mask = jnp.where((seg_block == prev_seg)[:, None], jnp.exp(cum_rate), 0.0)
    from_before = entry_mask[:, :, None] * jnp.einsum('thn,hpn->thp', c_heads, state_now, precision=highest)
    last_seg = seg_block[-1]
    weight = jnp.where((seg_block == last_seg)[:, None], jnp.exp(cum_rate[-1][None, :] - cum_rate), 0.0) * step_dt
    carried = jnp.where(last_seg == prev_seg, jnp.exp(cum_rate[-1]), 0.0)
    added_in = jnp.einsum('shp,shn->hpn', weight[:, :, None] * x_block.astype(jnp.float32), b_heads, precision=highest)
    return ((carried[:, None, None] * state_now + added_in, last_seg), in_block + from_before)

def to_blocks(values):
    return values.reshape((TOKENS // BLOCK, BLOCK) + values.shape[1:])

def reference(tokens, pack_source, segment_ids, w_in, w_dt, w_out, conv_x, conv_bc, dt_bias, decay_rate, skip_gain, norm_gain):
    packed = tokens[pack_source]
    projected = jnp.dot(packed, w_in, preferred_element_type=jnp.float32).astype(jnp.bfloat16)
    panels = projected.reshape(TOKENS, N_MP, PANEL)
    chan_width = DI // N_MP
    group_width = GN // N_MP
    x_in = panels[:, :, :chan_width].reshape(TOKENS, DI)
    z_in = panels[:, :, chan_width:2 * chan_width].reshape(TOKENS, DI)
    b_in = panels[:, :, 2 * chan_width:2 * chan_width + group_width].reshape(TOKENS, GN)
    c_in = panels[:, :, 2 * chan_width + group_width:].reshape(TOKENS, GN)
    dt_raw = jnp.dot(packed, w_dt, preferred_element_type=jnp.float32)
    stacked = jnp.concatenate([x_in, b_in, c_in], axis=1)
    kernel = jnp.concatenate([conv_x, conv_bc.reshape(CONV, 2 * GN)], axis=1)
    extended = jnp.concatenate([jnp.zeros((CONV - 1, DI + 2 * GN), jnp.bfloat16), stacked], axis=0)
    seg_ext = jnp.concatenate([jnp.full((CONV - 1,), -1, jnp.int32), segment_ids], axis=0)
    conv_sum = jnp.zeros((TOKENS, DI + 2 * GN), jnp.float32)
    for lag_index in range(CONV):
        same_seg = (seg_ext[lag_index:lag_index + TOKENS] == segment_ids)[:, None]
        conv_sum = conv_sum + jnp.where(same_seg, kernel[lag_index][None, :] * extended[lag_index:lag_index + TOKENS].astype(jnp.float32), 0.0)
    convolved = jax.nn.silu(conv_sum).astype(jnp.bfloat16)
    x_all = convolved[:, :DI].reshape(TOKENS, HEADS, HEAD_DIM)
    b_all = convolved[:, DI:DI + GN].reshape(TOKENS, GROUPS, STATE)
    c_all = convolved[:, DI + GN:].reshape(TOKENS, GROUPS, STATE)
    step_dt = jax.nn.softplus(dt_raw + dt_bias)
    step_rate = -step_dt * decay_rate
    initial = (jnp.zeros((HEADS, HEAD_DIM, STATE), jnp.float32), jnp.array(-1, jnp.int32))
    final, outputs = lax.scan(block_step, initial, (to_blocks(x_all), to_blocks(b_all), to_blocks(c_all), to_blocks(step_dt), to_blocks(step_rate), to_blocks(segment_ids)))
    scan_out = outputs.reshape(TOKENS, HEADS, HEAD_DIM) + skip_gain[None, :, None] * x_all.astype(jnp.float32)
    gated_out = scan_out.reshape(TOKENS, DI) * jax.nn.silu(z_in.astype(jnp.float32))
    grouped = gated_out.reshape(TOKENS, GROUPS, DI // GROUPS)
    inv_rms = lax.rsqrt(lax.optimization_barrier(jnp.mean(grouped * grouped, axis=2, keepdims=True)) + 1e-05)
    normed = ((grouped * inv_rms).reshape(TOKENS, DI) * norm_gain).astype(jnp.bfloat16)

    def add_panel(accum, panel_index):
        first_col = panel_index * chan_width
        left_part = lax.dynamic_slice_in_dim(normed, first_col, chan_width, 1)
        right_part = lax.dynamic_slice_in_dim(w_out, first_col, chan_width, 1)
        partial_sum = lax.dot_general(left_part, right_part, (((1,), (1,)), ((), ())), preferred_element_type=jnp.float32).astype(jnp.bfloat16)
        partial_sum = lax.optimization_barrier(partial_sum).astype(jnp.float32)
        return (accum + partial_sum, None)
    accum, _ = lax.scan(add_panel, jnp.zeros((TOKENS, D), jnp.float32), jnp.arange(N_MP, dtype=jnp.int32))
    return accum.astype(jnp.bfloat16)
```

```python
import jax
import jax.numpy as jnp
from jax import lax
from jax.experimental import pallas as pl
from jax.experimental.pallas import tpu as pltpu
from jax.sharding import PartitionSpec as P

HEAD_DIM = 64
STATE = 256
CONV = 4
BLOCK = 256


highest = lax.Precision.HIGHEST


def passed_along(x, axis, by):
    size = lax.axis_size(axis)
    pairs = [(i, i + by) for i in range(size) if 0 <= i + by < size]
    return lax.ppermute(x, axis, pairs)


def carried_in(x, axis, join, neutral):
    place = lax.axis_index(axis)
    gathered = jax.tree.map(
        lambda a, kind: lax.all_gather(a.astype(kind), axis), x, (jnp.bfloat16, jnp.bfloat16)
    )
    state = jax.tree.map(lambda a, e: jnp.zeros_like(a) + jnp.asarray(e, a.dtype), x, neutral)

    def one(hop, state):
        return join(
            state,
            jax.tree.map(
                lambda a, own: lax.dynamic_index_in_dim(a, hop, 0, False).astype(own.dtype),
                gathered,
                x,
            ),
        )

    return lax.fori_loop(0, place, one, state)


def chain_combine(earlier, later_part):
    return (earlier[0] * later_part[0], later_part[0][:, None, None] * earlier[1] + later_part[1])


def block_step(carry, pieces):
    state_now, prev_seg = carry
    x_block, b_block, c_block, step_dt, step_rate, seg_block = pieces
    per_group = x_block.shape[1] // b_block.shape[1]
    cum_rate = jnp.cumsum(step_rate, axis=0)
    places = jnp.arange(seg_block.shape[0])
    linked = (seg_block[:, None] == seg_block[None, :]) & (places[:, None] >= places[None, :])
    log_spans = cum_rate.T[:, :, None] - cum_rate.T[:, None, :]
    decay_mat = jnp.where(linked[None], jnp.exp(jnp.where(linked[None], log_spans, 0.0)), 0.0)
    scores = jnp.einsum("tgn,sgn->gts", c_block, b_block, preferred_element_type=jnp.float32)
    scores = jnp.repeat(scores, per_group, axis=0)
    mixing = (scores * decay_mat * step_dt.T[:, None, :]).astype(jnp.bfloat16)
    in_block = jnp.einsum("hts,shp->thp", mixing, x_block, preferred_element_type=jnp.float32)
    c_heads = jnp.repeat(c_block.astype(jnp.float32), per_group, axis=1)
    b_heads = jnp.repeat(b_block.astype(jnp.float32), per_group, axis=1)
    entry_mask = jnp.where((seg_block == prev_seg)[:, None], jnp.exp(cum_rate), 0.0)
    from_before = entry_mask[:, :, None] * jnp.einsum(
        "thn,hpn->thp", c_heads, state_now, precision=highest
    )
    last_seg = seg_block[-1]
    weight = (
        jnp.where((seg_block == last_seg)[:, None], jnp.exp(cum_rate[-1][None, :] - cum_rate), 0.0)
        * step_dt
    )
    carried = jnp.where(last_seg == prev_seg, jnp.exp(cum_rate[-1]), 0.0)
    added_in = jnp.einsum(
        "shp,shn->hpn", weight[:, :, None] * x_block.astype(jnp.float32), b_heads, precision=highest
    )
    return ((carried[:, None, None] * state_now + added_in, last_seg), in_block + from_before)


def on_device(
    tokens,
    pack_source,
    segment_ids,
    w_in,
    w_dt,
    w_out,
    conv_x,
    conv_bc,
    dt_bias,
    decay_rate,
    skip_gain,
    norm_gain,
):
    row_count = tokens.shape[0]
    data_devs = lax.axis_size("dp")
    capacity = 2 * row_count // data_devs
    source_dev = pack_source // row_count
    source_row = pack_source % row_count
    same_source = source_dev[:, None] == source_dev[None, :]
    earlier_rows = pack_source[None, :] < pack_source[:, None]
    rank_in = jnp.sum((same_source & earlier_rows).astype(jnp.int32), axis=1)
    slot_index = source_dev * capacity + rank_in
    requests = (
        jnp.full((data_devs * capacity,), -1, jnp.int32)
        .at[slot_index]
        .set(source_row)
        .reshape(data_devs, capacity)
    )
    wanted = lax.all_to_all(requests, "dp", split_axis=0, concat_axis=0, tiled=True)
    fetched = jnp.where(
        (wanted >= 0)[:, :, None], tokens[jnp.maximum(wanted, 0)], jnp.zeros((), jnp.bfloat16)
    )
    replies = lax.all_to_all(fetched, "dp", split_axis=0, concat_axis=0, tiled=True)
    gathered = replies.reshape(data_devs * capacity, tokens.shape[1])[slot_index]
    panel_cols = w_in.shape[1]
    head_count = w_dt.shape[1]
    chan_width = w_out.shape[1]
    proj_sum = jnp.dot(
        gathered, lax.all_gather(w_in, "dp", axis=0, tiled=True), preferred_element_type=jnp.float32
    )
    step_sum = jnp.dot(
        gathered, lax.all_gather(w_dt, "dp", axis=0, tiled=True), preferred_element_type=jnp.float32
    )
    proj_sum, dt_raw = (proj_sum, step_sum)
    projected = proj_sum.astype(jnp.bfloat16)
    group_width = (panel_cols - 2 * chan_width) // 2
    gate_in = projected[:, chan_width : 2 * chan_width]
    stacked = jnp.concatenate([projected[:, :chan_width], projected[:, 2 * chan_width :]], axis=1)
    tail_len = CONV - 1
    tail_vals = stacked[row_count - tail_len :].astype(jnp.float32)
    tail_seg = (segment_ids[row_count - tail_len :] + 1).astype(jnp.float32)
    prev_vals, prev_seg = passed_along((tail_vals, tail_seg), "dp", 1)
    extended = jnp.concatenate([prev_vals.astype(jnp.bfloat16), stacked], axis=0)
    seg_ext = jnp.concatenate([prev_seg.astype(jnp.int32) - 1, segment_ids], axis=0)
    kernel = jnp.concatenate([conv_x, conv_bc.reshape(CONV, 2 * group_width)], axis=1)
    conv_sum = jnp.zeros((row_count, stacked.shape[1]), jnp.float32)
    for lag_index in range(CONV):
        same_seg = (seg_ext[lag_index : lag_index + row_count] == segment_ids)[:, None]
        conv_sum = conv_sum + jnp.where(
            same_seg,
            kernel[lag_index][None, :]
            * extended[lag_index : lag_index + row_count].astype(jnp.float32),
            0.0,
        )
    convolved = jax.nn.silu(conv_sum).astype(jnp.bfloat16)
    local_groups = group_width // STATE
    x_all = convolved[:, :chan_width].reshape(row_count, head_count, HEAD_DIM)
    b_all = convolved[:, chan_width : chan_width + group_width].reshape(
        row_count, local_groups, STATE
    )
    c_all = convolved[:, chan_width + group_width :].reshape(row_count, local_groups, STATE)
    step_dt = jax.nn.softplus(dt_raw + dt_bias)
    step_rate = -step_dt * decay_rate
    seg_before = seg_ext[tail_len - 1]
    block_total = row_count // BLOCK

    def to_blocks(values):
        return values.reshape((block_total, BLOCK) + values.shape[1:])

    start_state = (jnp.zeros((head_count, HEAD_DIM, STATE), jnp.float32), seg_before)
    final, outputs = lax.scan(
        block_step,
        start_state,
        (
            to_blocks(x_all),
            to_blocks(b_all),
            to_blocks(c_all),
            to_blocks(step_dt),
            to_blocks(step_rate),
            to_blocks(segment_ids),
        ),
    )
    local_state = final[0]
    scan_out = outputs.reshape(row_count, head_count, HEAD_DIM)
    running = jnp.cumsum(step_rate, axis=0)
    carry_gain = jnp.where(segment_ids[-1] == seg_before, jnp.exp(running[-1]), 0.0)
    neutral = (jnp.ones((head_count,), jnp.float32), jnp.zeros_like(local_state))
    incoming = carried_in((carry_gain, local_state), "dp", chain_combine, neutral)[1]
    c_heads = jnp.repeat(c_all.astype(jnp.float32), head_count // local_groups, axis=1)
    entry_mask = jnp.where((segment_ids == seg_before)[:, None], jnp.exp(running), 0.0)
    scan_out = scan_out + entry_mask[:, :, None] * jnp.einsum(
        "thn,hpn->thp", c_heads, incoming, precision=highest
    )
    scan_out = scan_out + skip_gain[None, :, None] * x_all.astype(jnp.float32)
    gated_out = scan_out.reshape(row_count, chan_width) * jax.nn.silu(gate_in.astype(jnp.float32))
    grouped = gated_out.reshape(row_count, local_groups, chan_width // local_groups)
    inv_rms = lax.rsqrt(jnp.mean(grouped * grouped, axis=2, keepdims=True) + 1e-05)
    normed = ((grouped * inv_rms).reshape(row_count, chan_width) * norm_gain).astype(jnp.bfloat16)
    return lax.psum_scatter(
        lax.dot_general(
            normed, w_out, (((1,), (1,)), ((), ())), preferred_element_type=jnp.float32
        ).astype(jnp.bfloat16),
        "mp",
        scatter_dimension=0,
        tiled=True,
    )


HALO = 16
MESH = pl.DeviceIdType.MESH


def remote(src, dst, send, recv, dp):
    return pltpu.make_async_remote_copy(
        src_ref=src, dst_ref=dst, send_sem=send, recv_sem=recv,
        device_id={"dp": dp}, device_id_type=MESH,
    )


def projection_kernel(
    tok_hbm, meta_ref, w_hbm, wdt_ref,
    xb_out, dt_out, zc_out, meta_out,
    tokg, metas, wbuf, idxcol, onehot, packed, own,
    s_da, s_db, s_xa, s_yb, s_ya, s_xb,
    r_da, r_db, r_xa, r_yb, r_sa, r_sb,
    loc_sem, meta_send, meta_recv, w_send, w_recv,
    tok_send, tok_recv, fwd_send, fwd_recv, red_send, red_recv,
):
    me = lax.axis_index("dp")
    core = me % 2
    chip = me // 2
    at_x = chip % 2
    at_y = chip // 2
    chip_x = chip + 1 - 2 * at_x
    chip_y = chip + 2 - 4 * at_y
    chip_d = chip_x + chip_y - chip
    sibling = me + 1 - 2 * core
    rows, depth = tok_hbm.shape[0], w_hbm.shape[0]
    width = w_hbm.shape[1] // 5
    group, state = width, width // 4
    kdim = 2 * depth
    block = 2 * rows
    na = xb_out.shape[1]
    nb = zc_out.shape[1]

    barrier = pltpu.get_barrier_semaphore()
    for k in range(1, 8):
        pl.semaphore_signal(barrier, inc=1, device_id={"dp": (me + k) % 8}, device_id_type=MESH)
    pl.semaphore_wait(barrier, 7)

    mine = pl.ds(pl.multiple_of(me * rows, rows), rows)

    def columns(of_chip):
        return pl.ds(pl.multiple_of(of_chip * kdim, 128), kdim)

    copies = []
    for k in range(1, 8):
        copies.append(
            remote(meta_ref, metas.at[me], meta_send.at[k - 1], meta_recv.at[k - 1], (me + k) % 8)
        )
    directs = []
    for i, to in enumerate((chip_d, chip_x, chip_y)):
        directs.append(
            remote(tok_hbm.at[:, columns(to)], tokg.at[mine], tok_send.at[i], tok_recv.at[i],
                   2 * to + core)
        )
    for c in copies + directs:
        c.start()
    local = [
        pltpu.make_async_copy(tok_hbm.at[:, columns(chip)], tokg.at[mine], loc_sem.at[0]),
        pltpu.make_async_copy(meta_ref, metas.at[me], loc_sem.at[1]),
    ]
    forward = [
        remote(tok_hbm.at[:, columns(chip)], tokg.at[mine], fwd_send.at[0], fwd_recv.at[0], sibling)
    ]
    kmine = pl.ds(pl.multiple_of(core * depth, depth), depth)

    def pieces(g):
        return (
            (w_hbm.at[:, pl.ds(pl.multiple_of(g * group, 128), group)], 0, group),
            (w_hbm.at[:, pl.ds(pl.multiple_of(4 * group + g * state, 128), state)], group, state),
            (wdt_ref.at[g], na, 128),
            (w_hbm.at[:, pl.ds(pl.multiple_of(2 * group + g * group, 128), group)], na + 128, group),
            (w_hbm.at[:, pl.ds(pl.multiple_of(4 * group + 2 * state + g * state, 128), state)],
             na + 128 + group, state),
        )

    weights = []
    for i, (src, col, size) in enumerate(pieces(1 - core)):
        weights.append(
            remote(src, wbuf.at[kmine, pl.ds(col, size)], w_send.at[i], w_recv.at[i], sibling)
        )
    for i, (src, col, size) in enumerate(pieces(core)):
        local.append(
            pltpu.make_async_copy(src, wbuf.at[kmine, pl.ds(col, size)], loc_sem.at[2 + i])
        )
    for c in forward + weights + local:
        c.start()

    for c in copies:
        c.wait_recv()
    local[1].wait()
    idxcol[0:HALO, :] = jnp.full((HALO, 128), -1, jnp.int32)
    for j in range(8):
        row = metas[j, 0:1, :]
        idxcol[HALO + j * rows : HALO + (j + 1) * rows, :] = jnp.broadcast_to(row, (128, rows)).T
    meta_out[...] = metas[...]

    for i, source in enumerate((chip_d, chip_x, chip_y)):
        directs[i].wait_recv()
        theirs = pl.ds(pl.multiple_of((2 * source + core) * rows, rows), rows)
        c = remote(tokg.at[theirs], tokg.at[theirs], fwd_send.at[1 + i], fwd_recv.at[1 + i], sibling)
        c.start()
        forward.append(c)
    for c in local[:1] + local[2:]:
        c.wait()
    for c in weights + forward:
        c.wait_recv()

    lanes = lax.broadcasted_iota(jnp.int32, (block + HALO, 128), 1)

    def pack(of_chip, slot):
        ids = idxcol[pl.ds(pl.multiple_of(of_chip * block, block), block + HALO), :]

        @pl.loop(0, 8 * rows // 128)
        def _(t):
            onehot[:, pl.ds(pl.multiple_of(t * 128, 128), 128)] = jnp.where(
                ids == lanes + t * 128, 1.0, 0.0
            ).astype(jnp.bfloat16)

        @pl.loop(0, kdim // 256)
        def _(t):
            cols = pl.ds(pl.multiple_of(t * 256, 256), 256)
            packed[slot, :, cols] = jnp.dot(
                onehot[...], tokg[:, cols], preferred_element_type=jnp.float32
            ).astype(jnp.bfloat16)

    def product(slot, col, size):
        return jnp.dot(
            packed[slot], wbuf[:, pl.ds(col, size)], preferred_element_type=jnp.float32
        )

    def split(acc):
        high = acc.astype(jnp.bfloat16).astype(jnp.float32)
        return jnp.where(lanes < 16, high, acc - high).astype(jnp.bfloat16)

    def joined(ref):
        r = ref[:, na : na + 128].astype(jnp.float32)
        return r + jnp.where(lanes < 16, pltpu.roll(r, 112, 1), pltpu.roll(r, 16, 1))

    def part_a(slot, out, add=None):
        @pl.loop(0, na // 256)
        def _(t):
            col = pl.multiple_of(t * 256, 256)
            acc = product(slot, col, 256)
            if add is not None:
                acc = acc + add[:, pl.ds(col, 256)].astype(jnp.float32)
            out[:, pl.ds(col, 256)] = acc.astype(jnp.bfloat16)

        acc = product(slot, na, 128)
        if add is not None:
            acc = acc + joined(add)
        out[:, na : na + 128] = split(acc)

    def part_b(slot, out, add=None):
        @pl.loop(0, nb // 256)
        def _(t):
            col = pl.multiple_of(t * 256, 256)
            acc = product(slot, pl.multiple_of(na + 128 + col, 128), 256)
            if add is not None:
                acc = acc + add[:, pl.ds(col, 256)].astype(jnp.float32)
            out[:, pl.ds(col, 256)] = acc.astype(jnp.bfloat16)

    dev_x, dev_y = 2 * chip_x + core, 2 * chip_y + core
    c_da = remote(s_da, r_da, red_send.at[0], red_recv.at[0], dev_x)
    c_db = remote(s_db, r_db, red_send.at[1], red_recv.at[1], dev_y)
    c_xa = remote(s_xa, r_xa, red_send.at[2], red_recv.at[2], dev_x)
    c_yb = remote(s_yb, r_yb, red_send.at[3], red_recv.at[3], dev_y)
    c_ya = remote(s_ya, r_sa, red_send.at[4], red_recv.at[4], dev_y)
    c_xb = remote(s_xb, r_sb, red_send.at[5], red_recv.at[5], dev_x)
    pack(chip_d, 0)
    part_a(0, s_da)
    c_da.start()
    part_b(0, s_db)
    c_db.start()
    pack(chip_x, 1)
    part_a(1, s_xa)
    c_xa.start()
    pack(chip_y, 2)
    part_b(2, s_yb)
    c_yb.start()
    pack(chip, 0)

    @pl.loop(0, na // 256)
    def _(t):
        col = pl.multiple_of(t * 256, 256)
        own[:, pl.ds(col, 256)] = product(0, col, 256)

    own[:, na : na + 128] = product(0, na, 128)

    @pl.loop(0, nb // 256)
    def _(t):
        col = pl.multiple_of(na + 128 + t * 256, 128)
        own[:, pl.ds(col, 256)] = product(0, col, 256)

    c_da.wait_recv()
    part_a(2, s_ya, r_da)
    c_ya.start()
    c_db.wait_recv()
    part_b(1, s_xb, r_db)
    c_xb.start()
    c_xa.wait_recv()
    c_yb.wait_recv()
    c_ya.wait_recv()

    @pl.loop(0, na // 256)
    def _(t):
        cols = pl.ds(pl.multiple_of(t * 256, 256), 256)
        xb_out[:, cols] = (
            own[:, cols] + r_xa[:, cols].astype(jnp.float32) + r_sa[:, cols].astype(jnp.float32)
        ).astype(jnp.bfloat16)

    dt_out[...] = own[:, na : na + 128] + joined(r_xa) + joined(r_sa)
    c_xb.wait_recv()

    @pl.loop(0, nb // 256)
    def _(t):
        cols = pl.ds(pl.multiple_of(t * 256, 256), 256)
        own_cols = pl.ds(pl.multiple_of(na + 128 + t * 256, 128), 256)
        zc_out[:, cols] = (
            own[:, own_cols] + r_yb[:, cols].astype(jnp.float32) + r_sb[:, cols].astype(jnp.float32)
        ).astype(jnp.bfloat16)

    for c in copies + directs + forward + weights + [c_da, c_db, c_xa, c_yb, c_ya, c_xb]:
        c.wait_send()


def project(tokens, meta, w_in, wdt):
    rows, depth = tokens.shape[0], w_in.shape[0]
    width = w_in.shape[1] // 5
    na = width + width // 4
    nb = na
    m = 2 * rows + HALO
    bf = jnp.bfloat16
    vmem = pl.BlockSpec(memory_space=pltpu.VMEM)
    hbm = pl.BlockSpec(memory_space=pl.ANY)
    dma = pltpu.SemaphoreType.DMA
    a, b = pltpu.VMEM((m, na + 128), bf), pltpu.VMEM((m, nb), bf)
    return pl.pallas_call(
        projection_kernel,
        out_shape=(
            jax.ShapeDtypeStruct((m, na), bf),
            jax.ShapeDtypeStruct((m, 128), jnp.float32),
            jax.ShapeDtypeStruct((m, nb), bf),
            jax.ShapeDtypeStruct((8, 8, rows), jnp.int32),
        ),
        in_specs=[hbm, vmem, hbm, vmem],
        out_specs=(vmem,) * 4,
        scratch_shapes=[
            pltpu.VMEM((8 * rows, 2 * depth), bf),
            pltpu.VMEM((8, 8, rows), jnp.int32),
            pltpu.VMEM((2 * depth, na + 128 + nb), bf),
            pltpu.VMEM((8 * rows + HALO, 128), jnp.int32),
            pltpu.VMEM((m, 8 * rows), bf),
            pltpu.VMEM((3, m, 2 * depth), bf),
            pltpu.VMEM((m, na + 128 + nb), jnp.float32),
            a, b, a, b, a, b,
            a, b, a, b, a, b,
            dma((7,)), dma((7,)), dma((7,)), dma((5,)), dma((5,)),
            dma((3,)), dma((3,)), dma((4,)), dma((4,)), dma((6,)), dma((6,)),
        ],
        compiler_params=pltpu.CompilerParams(
            collective_id=0, has_side_effects=True, vmem_limit_bytes=58 << 20
        ),
    )(tokens, meta, w_in, wdt)


def on_plane(
    tokens, pack_source, segment_ids, w_in, w_dt, w_out, conv_x, conv_bc,
    dt_bias, decay_rate, skip_gain, norm_gain,
):
    f32, bf = jnp.float32, jnp.bfloat16
    rows = tokens.shape[0]
    total = 8 * rows
    block = 2 * rows
    me = lax.axis_index("dp")
    core, chip = me % 2, me // 2
    heads = w_dt.shape[1] // 2
    chans = w_out.shape[1] // 2

    def mine(values, axis):
        size = values.shape[axis] // 2
        return lax.dynamic_slice_in_dim(values, core * size, size, axis)

    meta = jnp.pad(jnp.stack([pack_source, segment_ids]), ((0, 6), (0, 0)))
    halves = w_dt.reshape(w_dt.shape[0], 2, heads).transpose(1, 0, 2)
    wdt = jnp.pad(jnp.concatenate([halves, halves], axis=2), ((0, 0), (0, 0), (0, 128 - 2 * heads)))
    xb, dt_raw, zc, metas = project(tokens, meta, w_in, wdt)
    seg_all = jnp.concatenate([jnp.full((HALO,), -1, jnp.int32), metas[:, 1, :].reshape(total)])
    seg_ext = lax.dynamic_slice_in_dim(seg_all, chip * block, block + HALO, 0)
    seg = seg_ext[HALO:]
    seg_before = seg_ext[HALO - 1]
    taps_bc = mine(conv_bc, 2)

    def convolve(values, taps):
        total_sum = jnp.zeros((block, values.shape[1]), f32)
        for lag in range(CONV):
            first = HALO - CONV + 1 + lag
            same = (seg_ext[first : first + block] == seg)[:, None]
            total_sum = total_sum + jnp.where(
                same, taps[lag][None, :] * values[first : first + block].astype(f32), 0.0
            )
        return jax.nn.silu(total_sum).astype(bf)

    x = convolve(xb[:, :chans], mine(conv_x, 1))
    b = convolve(xb[:, chans:], taps_bc[:, 0])
    c = convolve(zc[:, chans:], taps_bc[:, 1])
    gate = jax.nn.silu(zc[HALO:, :chans].astype(f32))
    step_dt = jax.nn.softplus(dt_raw[HALO:, :heads] + mine(dt_bias, 0))
    step_rate = -step_dt * mine(decay_rate, 0)
    places = jnp.arange(block)
    lower = (places[:, None] >= places[None, :])
    cum = jnp.dot(lower.astype(f32), step_rate, precision=highest)
    xh = x.reshape(block, heads, HEAD_DIM)

    last = seg[-1]
    weight = jnp.where((seg == last)[:, None], jnp.exp(cum[-1][None, :] - cum), 0.0) * step_dt
    wide = jnp.repeat(weight, HEAD_DIM, axis=1)
    weighted = (wide * x.astype(f32)).astype(bf)
    left = lax.dot_general(weighted, b, (((0,), (0,)), ((), ())), preferred_element_type=f32)
    gain = jnp.where(last == seg_before, jnp.exp(cum[-1]), 0.0)
    sent = jnp.concatenate(
        [left.reshape(heads, HEAD_DIM * STATE), jnp.broadcast_to(gain[:, None], (heads, 128))], axis=1
    ).astype(bf)
    groups = [[i, i + 2, i + 4, i + 6] for i in range(2)]
    gathered = lax.all_gather(sent, "dp", axis_index_groups=groups).astype(f32)

    linked = (seg[:, None] == seg[None, :]) & lower
    cum_t = cum.T
    spans = cum_t[:, :, None] - cum_t[:, None, :]
    decay = jnp.where(linked[None], jnp.exp(jnp.where(linked[None], spans, 0.0)), 0.0)
    scores = lax.dot_general(c, b, (((1,), (1,)), ((), ())), preferred_element_type=f32)
    mixing = (scores[None] * decay * step_dt.T[:, None, :]).astype(bf)
    ssd = jnp.einsum("hts,shp->thp", mixing, xh, preferred_element_type=f32).reshape(block, chans)

    incoming = jnp.zeros((heads, HEAD_DIM * STATE), f32)
    for k in range(3):
        part = gathered[k]
        incoming = jnp.where(
            k < chip, part[:, -1:] * incoming + part[:, : HEAD_DIM * STATE], incoming
        )
    before = incoming.reshape(chans, STATE).astype(bf)
    entry = jnp.where((seg == seg_before)[:, None], jnp.exp(cum), 0.0)
    ssd = ssd + jnp.repeat(entry, HEAD_DIM, axis=1) * lax.dot_general(
        c, before, (((1,), (1,)), ((), ())), preferred_element_type=f32
    )
    skip = jnp.repeat(mine(skip_gain, 0), HEAD_DIM)[None, :]
    gated = (ssd + skip * x.astype(f32)) * gate
    inv = lax.rsqrt(jnp.mean(gated * gated, axis=1, keepdims=True) + 1e-05)
    normed = (gated * inv * mine(norm_gain, 0)[None, :]).astype(bf)

    keep = lax.dynamic_slice_in_dim(normed, core * rows, rows, 0)
    give = lax.dynamic_slice_in_dim(normed, (1 - core) * rows, rows, 0)
    got = lax.ppermute(give, "dp", [(i, i + 1 - 2 * (i % 2)) for i in range(8)])
    whole = jnp.where(
        core == 0, jnp.concatenate([keep, got], axis=1), jnp.concatenate([got, keep], axis=1)
    )
    return lax.psum_scatter(
        lax.dot_general(
            whole, w_out, (((1,), (1,)), ((), ())), preferred_element_type=f32
        ).astype(bf),
        "mp",
        scatter_dimension=0,
        tiled=True,
    )


def solution(mesh):
    placed = (
        P("dp", None),
        P("dp"),
        P("dp"),
        P("dp", "mp"),
        P("dp", "mp"),
        P(None, "mp"),
        P(None, "mp"),
        P(None, None, "mp"),
        P("mp"),
        P("mp"),
        P("mp"),
        P("mp"),
    )
    body = on_plane if mesh.shape["dp"] == 8 else on_device
    return jax.shard_map(
        body, mesh=mesh, in_specs=placed, out_specs=P(("dp", "mp"), None), check_vma=False
    )
```

```python
import jax
import jax.numpy as jnp
from jax import lax
from jax.experimental import pallas as pl
from jax.experimental.pallas import tpu as pltpu
from jax.sharding import PartitionSpec as P

HEAD_DIM = 64
STATE = 256
CONV = 4
BLOCK = 256


highest = lax.Precision.HIGHEST


def passed_along(x, axis, by):
    size = lax.axis_size(axis)
    pairs = [(i, i + by) for i in range(size) if 0 <= i + by < size]
    return lax.ppermute(x, axis, pairs)


def carried_in(x, axis, join, neutral):
    place = lax.axis_index(axis)
    gathered = jax.tree.map(
        lambda a, kind: lax.all_gather(a.astype(kind), axis), x, (jnp.bfloat16, jnp.bfloat16)
    )
    state = jax.tree.map(lambda a, e: jnp.zeros_like(a) + jnp.asarray(e, a.dtype), x, neutral)

    def one(hop, state):
        return join(
            state,
            jax.tree.map(
                lambda a, own: lax.dynamic_index_in_dim(a, hop, 0, False).astype(own.dtype),
                gathered,
                x,
            ),
        )

    return lax.fori_loop(0, place, one, state)


def chain_combine(earlier, later_part):
    return (earlier[0] * later_part[0], later_part[0][:, None, None] * earlier[1] + later_part[1])


def block_step(carry, pieces):
    state_now, prev_seg = carry
    x_block, b_block, c_block, step_dt, step_rate, seg_block = pieces
    per_group = x_block.shape[1] // b_block.shape[1]
    cum_rate = jnp.cumsum(step_rate, axis=0)
    places = jnp.arange(seg_block.shape[0])
    linked = (seg_block[:, None] == seg_block[None, :]) & (places[:, None] >= places[None, :])
    log_spans = cum_rate.T[:, :, None] - cum_rate.T[:, None, :]
    decay_mat = jnp.where(linked[None], jnp.exp(jnp.where(linked[None], log_spans, 0.0)), 0.0)
    scores = jnp.einsum("tgn,sgn->gts", c_block, b_block, preferred_element_type=jnp.float32)
    scores = jnp.repeat(scores, per_group, axis=0)
    mixing = (scores * decay_mat * step_dt.T[:, None, :]).astype(jnp.bfloat16)
    in_block = jnp.einsum("hts,shp->thp", mixing, x_block, preferred_element_type=jnp.float32)
    c_heads = jnp.repeat(c_block.astype(jnp.float32), per_group, axis=1)
    b_heads = jnp.repeat(b_block.astype(jnp.float32), per_group, axis=1)
    entry_mask = jnp.where((seg_block == prev_seg)[:, None], jnp.exp(cum_rate), 0.0)
    from_before = entry_mask[:, :, None] * jnp.einsum(
        "thn,hpn->thp", c_heads, state_now, precision=highest
    )
    last_seg = seg_block[-1]
    weight = (
        jnp.where((seg_block == last_seg)[:, None], jnp.exp(cum_rate[-1][None, :] - cum_rate), 0.0)
        * step_dt
    )
    carried = jnp.where(last_seg == prev_seg, jnp.exp(cum_rate[-1]), 0.0)
    added_in = jnp.einsum(
        "shp,shn->hpn", weight[:, :, None] * x_block.astype(jnp.float32), b_heads, precision=highest
    )
    return ((carried[:, None, None] * state_now + added_in, last_seg), in_block + from_before)


def on_device(
    tokens,
    pack_source,
    segment_ids,
    w_in,
    w_dt,
    w_out,
    conv_x,
    conv_bc,
    dt_bias,
    decay_rate,
    skip_gain,
    norm_gain,
):
    row_count = tokens.shape[0]
    data_devs = lax.axis_size("dp")
    capacity = 2 * row_count // data_devs
    source_dev = pack_source // row_count
    source_row = pack_source % row_count
    same_source = source_dev[:, None] == source_dev[None, :]
    earlier_rows = pack_source[None, :] < pack_source[:, None]
    rank_in = jnp.sum((same_source & earlier_rows).astype(jnp.int32), axis=1)
    slot_index = source_dev * capacity + rank_in
    requests = (
        jnp.full((data_devs * capacity,), -1, jnp.int32)
        .at[slot_index]
        .set(source_row)
        .reshape(data_devs, capacity)
    )
    wanted = lax.all_to_all(requests, "dp", split_axis=0, concat_axis=0, tiled=True)
    fetched = jnp.where(
        (wanted >= 0)[:, :, None], tokens[jnp.maximum(wanted, 0)], jnp.zeros((), jnp.bfloat16)
    )
    replies = lax.all_to_all(fetched, "dp", split_axis=0, concat_axis=0, tiled=True)
    gathered = replies.reshape(data_devs * capacity, tokens.shape[1])[slot_index]
    panel_cols = w_in.shape[1]
    head_count = w_dt.shape[1]
    chan_width = w_out.shape[1]
    proj_sum = jnp.dot(
        gathered, lax.all_gather(w_in, "dp", axis=0, tiled=True), preferred_element_type=jnp.float32
    )
    step_sum = jnp.dot(
        gathered, lax.all_gather(w_dt, "dp", axis=0, tiled=True), preferred_element_type=jnp.float32
    )
    proj_sum, dt_raw = (proj_sum, step_sum)
    projected = proj_sum.astype(jnp.bfloat16)
    group_width = (panel_cols - 2 * chan_width) // 2
    gate_in = projected[:, chan_width : 2 * chan_width]
    stacked = jnp.concatenate([projected[:, :chan_width], projected[:, 2 * chan_width :]], axis=1)
    tail_len = CONV - 1
    tail_vals = stacked[row_count - tail_len :].astype(jnp.float32)
    tail_seg = (segment_ids[row_count - tail_len :] + 1).astype(jnp.float32)
    prev_vals, prev_seg = passed_along((tail_vals, tail_seg), "dp", 1)
    extended = jnp.concatenate([prev_vals.astype(jnp.bfloat16), stacked], axis=0)
    seg_ext = jnp.concatenate([prev_seg.astype(jnp.int32) - 1, segment_ids], axis=0)
    kernel = jnp.concatenate([conv_x, conv_bc.reshape(CONV, 2 * group_width)], axis=1)
    conv_sum = jnp.zeros((row_count, stacked.shape[1]), jnp.float32)
    for lag_index in range(CONV):
        same_seg = (seg_ext[lag_index : lag_index + row_count] == segment_ids)[:, None]
        conv_sum = conv_sum + jnp.where(
            same_seg,
            kernel[lag_index][None, :]
            * extended[lag_index : lag_index + row_count].astype(jnp.float32),
            0.0,
        )
    convolved = jax.nn.silu(conv_sum).astype(jnp.bfloat16)
    local_groups = group_width // STATE
    x_all = convolved[:, :chan_width].reshape(row_count, head_count, HEAD_DIM)
    b_all = convolved[:, chan_width : chan_width + group_width].reshape(
        row_count, local_groups, STATE
    )
    c_all = convolved[:, chan_width + group_width :].reshape(row_count, local_groups, STATE)
    step_dt = jax.nn.softplus(dt_raw + dt_bias)
    step_rate = -step_dt * decay_rate
    seg_before = seg_ext[tail_len - 1]
    block_total = row_count // BLOCK

    def to_blocks(values):
        return values.reshape((block_total, BLOCK) + values.shape[1:])

    start_state = (jnp.zeros((head_count, HEAD_DIM, STATE), jnp.float32), seg_before)
    final, outputs = lax.scan(
        block_step,
        start_state,
        (
            to_blocks(x_all),
            to_blocks(b_all),
            to_blocks(c_all),
            to_blocks(step_dt),
            to_blocks(step_rate),
            to_blocks(segment_ids),
        ),
    )
    local_state = final[0]
    scan_out = outputs.reshape(row_count, head_count, HEAD_DIM)
    running = jnp.cumsum(step_rate, axis=0)
    carry_gain = jnp.where(segment_ids[-1] == seg_before, jnp.exp(running[-1]), 0.0)
    neutral = (jnp.ones((head_count,), jnp.float32), jnp.zeros_like(local_state))
    incoming = carried_in((carry_gain, local_state), "dp", chain_combine, neutral)[1]
    c_heads = jnp.repeat(c_all.astype(jnp.float32), head_count // local_groups, axis=1)
    entry_mask = jnp.where((segment_ids == seg_before)[:, None], jnp.exp(running), 0.0)
    scan_out = scan_out + entry_mask[:, :, None] * jnp.einsum(
        "thn,hpn->thp", c_heads, incoming, precision=highest
    )
    scan_out = scan_out + skip_gain[None, :, None] * x_all.astype(jnp.float32)
    gated_out = scan_out.reshape(row_count, chan_width) * jax.nn.silu(gate_in.astype(jnp.float32))
    grouped = gated_out.reshape(row_count, local_groups, chan_width // local_groups)
    inv_rms = lax.rsqrt(jnp.mean(grouped * grouped, axis=2, keepdims=True) + 1e-05)
    normed = ((grouped * inv_rms).reshape(row_count, chan_width) * norm_gain).astype(jnp.bfloat16)
    return lax.psum_scatter(
        lax.dot_general(
            normed, w_out, (((1,), (1,)), ((), ())), preferred_element_type=jnp.float32
        ).astype(jnp.bfloat16),
        "mp",
        scatter_dimension=0,
        tiled=True,
    )


HALO = 16
MESH = pl.DeviceIdType.MESH


def remote(src, dst, send, recv, dp):
    return pltpu.make_async_remote_copy(
        src_ref=src, dst_ref=dst, send_sem=send, recv_sem=recv,
        device_id={"dp": dp}, device_id_type=MESH,
    )


def projection_kernel(
    tok_hbm, meta_ref, w_hbm, wdt_ref,
    xb_out, dt_out, zc_out, meta_out,
    tokg, metas, wbuf, idxcol, onehot, packed, own,
    s_da, s_db, s_xa, s_yb, s_ya, s_xb,
    r_da, r_db, r_xa, r_yb, r_sa, r_sb,
    loc_sem, meta_send, meta_recv, w_send, w_recv,
    tok_send, tok_recv, fwd_send, fwd_recv, red_send, red_recv,
):
    me = lax.axis_index("dp")
    core = me % 2
    chip = me // 2
    at_x = chip % 2
    at_y = chip // 2
    chip_x = chip + 1 - 2 * at_x
    chip_y = chip + 2 - 4 * at_y
    chip_d = chip_x + chip_y - chip
    sibling = me + 1 - 2 * core
    rows, depth = tok_hbm.shape[0], w_hbm.shape[0]
    width = w_hbm.shape[1] // 5
    group, state = width, width // 4
    kdim = 2 * depth
    block = 2 * rows
    na = xb_out.shape[1]
    nb = zc_out.shape[1]

    barrier = pltpu.get_barrier_semaphore()
    for k in range(1, 8):
        pl.semaphore_signal(barrier, inc=1, device_id={"dp": (me + k) % 8}, device_id_type=MESH)
    pl.semaphore_wait(barrier, 7)

    mine = pl.ds(pl.multiple_of(me * rows, rows), rows)

    def columns(of_chip):
        return pl.ds(pl.multiple_of(of_chip * kdim, 128), kdim)

    copies = []
    for k in range(1, 8):
        copies.append(
            remote(meta_ref, metas.at[me], meta_send.at[k - 1], meta_recv.at[k - 1], (me + k) % 8)
        )
    directs = []
    for i, to in enumerate((chip_d, chip_x, chip_y)):
        directs.append(
            remote(tok_hbm.at[:, columns(to)], tokg.at[mine], tok_send.at[i], tok_recv.at[i],
                   2 * to + core)
        )
    for c in copies + directs:
        c.start()
    local = [
        pltpu.make_async_copy(tok_hbm.at[:, columns(chip)], tokg.at[mine], loc_sem.at[0]),
        pltpu.make_async_copy(meta_ref, metas.at[me], loc_sem.at[1]),
    ]
    forward = [
        remote(tok_hbm.at[:, columns(chip)], tokg.at[mine], fwd_send.at[0], fwd_recv.at[0], sibling)
    ]
    kmine = pl.ds(pl.multiple_of(core * depth, depth), depth)

    def pieces(g):
        return (
            (w_hbm.at[:, pl.ds(pl.multiple_of(g * group, 128), group)], 0, group),
            (w_hbm.at[:, pl.ds(pl.multiple_of(4 * group + g * state, 128), state)], group, state),
            (wdt_ref.at[g], na, 128),
            (w_hbm.at[:, pl.ds(pl.multiple_of(2 * group + g * group, 128), group)], na + 128, group),
            (w_hbm.at[:, pl.ds(pl.multiple_of(4 * group + 2 * state + g * state, 128), state)],
             na + 128 + group, state),
        )

    weights = []
    for i, (src, col, size) in enumerate(pieces(1 - core)):
        weights.append(
            remote(src, wbuf.at[kmine, pl.ds(col, size)], w_send.at[i], w_recv.at[i], sibling)
        )
    for i, (src, col, size) in enumerate(pieces(core)):
        local.append(
            pltpu.make_async_copy(src, wbuf.at[kmine, pl.ds(col, size)], loc_sem.at[2 + i])
        )
    for c in forward + weights + local:
        c.start()

    for c in copies:
        c.wait_recv()
    local[1].wait()
    idxcol[0:HALO, :] = jnp.full((HALO, 128), -1, jnp.int32)
    for j in range(8):
        row = metas[j, 0:1, :]
        idxcol[HALO + j * rows : HALO + (j + 1) * rows, :] = jnp.broadcast_to(row, (128, rows)).T
    meta_out[...] = metas[...]

    for i, source in enumerate((chip_d, chip_x, chip_y)):
        directs[i].wait_recv()
        theirs = pl.ds(pl.multiple_of((2 * source + core) * rows, rows), rows)
        c = remote(tokg.at[theirs], tokg.at[theirs], fwd_send.at[1 + i], fwd_recv.at[1 + i], sibling)
        c.start()
        forward.append(c)
    for c in local[:1] + local[2:]:
        c.wait()
    for c in weights + forward:
        c.wait_recv()

    lanes = lax.broadcasted_iota(jnp.int32, (block + HALO, 128), 1)

    def pack(of_chip, slot):
        ids = idxcol[pl.ds(pl.multiple_of(of_chip * block, block), block + HALO), :]

        @pl.loop(0, 8 * rows // 128)
        def _(t):
            onehot[:, pl.ds(pl.multiple_of(t * 128, 128), 128)] = jnp.where(
                ids == lanes + t * 128, 1.0, 0.0
            ).astype(jnp.bfloat16)

        @pl.loop(0, kdim // 256)
        def _(t):
            cols = pl.ds(pl.multiple_of(t * 256, 256), 256)
            packed[slot, :, cols] = jnp.dot(
                onehot[...], tokg[:, cols], preferred_element_type=jnp.float32
            ).astype(jnp.bfloat16)

    def product(slot, col, size):
        return jnp.dot(
            packed[slot], wbuf[:, pl.ds(col, size)], preferred_element_type=jnp.float32
        )

    def split(acc):
        high = acc.astype(jnp.bfloat16).astype(jnp.float32)
        return jnp.where(lanes < 16, high, acc - high).astype(jnp.bfloat16)

    def joined(ref):
        r = ref[:, na : na + 128].astype(jnp.float32)
        return r + jnp.where(lanes < 16, pltpu.roll(r, 112, 1), pltpu.roll(r, 16, 1))

    def part_a(slot, out, add=None):
        @pl.loop(0, na // 256)
        def _(t):
            col = pl.multiple_of(t * 256, 256)
            acc = product(slot, col, 256)
            if add is not None:
                acc = acc + add[:, pl.ds(col, 256)].astype(jnp.float32)
            out[:, pl.ds(col, 256)] = acc.astype(jnp.bfloat16)

        acc = product(slot, na, 128)
        if add is not None:
            acc = acc + joined(add)
        out[:, na : na + 128] = split(acc)

    def part_b(slot, out, add=None):
        @pl.loop(0, nb // 256)
        def _(t):
            col = pl.multiple_of(t * 256, 256)
            acc = product(slot, pl.multiple_of(na + 128 + col, 128), 256)
            if add is not None:
                acc = acc + add[:, pl.ds(col, 256)].astype(jnp.float32)
            out[:, pl.ds(col, 256)] = acc.astype(jnp.bfloat16)

    dev_x, dev_y = 2 * chip_x + core, 2 * chip_y + core
    c_da = remote(s_da, r_da, red_send.at[0], red_recv.at[0], dev_x)
    c_db = remote(s_db, r_db, red_send.at[1], red_recv.at[1], dev_y)
    c_xa = remote(s_xa, r_xa, red_send.at[2], red_recv.at[2], dev_x)
    c_yb = remote(s_yb, r_yb, red_send.at[3], red_recv.at[3], dev_y)
    c_ya = remote(s_ya, r_sa, red_send.at[4], red_recv.at[4], dev_y)
    c_xb = remote(s_xb, r_sb, red_send.at[5], red_recv.at[5], dev_x)
    pack(chip_d, 0)
    part_a(0, s_da)
    c_da.start()
    part_b(0, s_db)
    c_db.start()
    pack(chip_x, 1)
    part_a(1, s_xa)
    c_xa.start()
    pack(chip_y, 2)
    part_b(2, s_yb)
    c_yb.start()
    pack(chip, 0)

    @pl.loop(0, na // 256)
    def _(t):
        col = pl.multiple_of(t * 256, 256)
        own[:, pl.ds(col, 256)] = product(0, col, 256)

    own[:, na : na + 128] = product(0, na, 128)

    @pl.loop(0, nb // 256)
    def _(t):
        col = pl.multiple_of(na + 128 + t * 256, 128)
        own[:, pl.ds(col, 256)] = product(0, col, 256)

    c_da.wait_recv()
    part_a(2, s_ya, r_da)
    c_ya.start()
    c_db.wait_recv()
    part_b(1, s_xb, r_db)
    c_xb.start()
    c_xa.wait_recv()
    c_yb.wait_recv()
    c_ya.wait_recv()

    @pl.loop(0, na // 256)
    def _(t):
        cols = pl.ds(pl.multiple_of(t * 256, 256), 256)
        xb_out[:, cols] = (
            own[:, cols] + r_xa[:, cols].astype(jnp.float32) + r_sa[:, cols].astype(jnp.float32)
        ).astype(jnp.bfloat16)

    dt_out[...] = own[:, na : na + 128] + joined(r_xa) + joined(r_sa)
    c_xb.wait_recv()

    @pl.loop(0, nb // 256)
    def _(t):
        cols = pl.ds(pl.multiple_of(t * 256, 256), 256)
        own_cols = pl.ds(pl.multiple_of(na + 128 + t * 256, 128), 256)
        zc_out[:, cols] = (
            own[:, own_cols] + r_yb[:, cols].astype(jnp.float32) + r_sb[:, cols].astype(jnp.float32)
        ).astype(jnp.bfloat16)

    for c in copies + directs + forward + weights + [c_da, c_db, c_xa, c_yb, c_ya, c_xb]:
        c.wait_send()


def project(tokens, meta, w_in, wdt):
    rows, depth = tokens.shape[0], w_in.shape[0]
    width = w_in.shape[1] // 5
    na = width + width // 4
    nb = na
    m = 2 * rows + HALO
    bf = jnp.bfloat16
    vmem = pl.BlockSpec(memory_space=pltpu.VMEM)
    hbm = pl.BlockSpec(memory_space=pl.ANY)
    dma = pltpu.SemaphoreType.DMA
    a, b = pltpu.VMEM((m, na + 128), bf), pltpu.VMEM((m, nb), bf)
    return pl.pallas_call(
        projection_kernel,
        out_shape=(
            jax.ShapeDtypeStruct((m, na), bf),
            jax.ShapeDtypeStruct((m, 128), jnp.float32),
            jax.ShapeDtypeStruct((m, nb), bf),
            jax.ShapeDtypeStruct((8, 8, rows), jnp.int32),
        ),
        in_specs=[hbm, vmem, hbm, vmem],
        out_specs=(vmem,) * 4,
        scratch_shapes=[
            pltpu.VMEM((8 * rows, 2 * depth), bf),
            pltpu.VMEM((8, 8, rows), jnp.int32),
            pltpu.VMEM((2 * depth, na + 128 + nb), bf),
            pltpu.VMEM((8 * rows + HALO, 128), jnp.int32),
            pltpu.VMEM((m, 8 * rows), bf),
            pltpu.VMEM((3, m, 2 * depth), bf),
            pltpu.VMEM((m, na + 128 + nb), jnp.float32),
            a, b, a, b, a, b,
            a, b, a, b, a, b,
            dma((7,)), dma((7,)), dma((7,)), dma((5,)), dma((5,)),
            dma((3,)), dma((3,)), dma((4,)), dma((4,)), dma((6,)), dma((6,)),
        ],
        compiler_params=pltpu.CompilerParams(
            collective_id=0, has_side_effects=True, vmem_limit_bytes=58 << 20
        ),
    )(tokens, meta, w_in, wdt)


TILES = 4


def output_kernel(normed_ref, w_hbm, out_ref, whole, wbuf, own, sent, got,
                  loc_sem, sib_send, sib_recv, send_sem, recv_sem):
    dp, m = lax.axis_index("dp"), lax.axis_index("mp")
    core = dp % 2
    sibling = dp + 1 - 2 * core
    half = normed_ref.shape[0] // 2
    chans = normed_ref.shape[1]
    part = half // 4
    step = w_hbm.shape[0] // TILES

    barrier = pltpu.get_barrier_semaphore()
    pl.semaphore_signal(barrier, inc=1, device_id={"dp": sibling}, device_id_type=MESH)
    for k in range(1, 4):
        pl.semaphore_signal(barrier, inc=1, device_id={"mp": (m + k) % 4}, device_id_type=MESH)
    loads = []
    for t in range(TILES):
        rows = pl.ds(t * step, step)
        loads.append(pltpu.make_async_copy(w_hbm.at[rows], wbuf.at[rows], loc_sem.at[t]))
        loads[t].start()
    pl.semaphore_wait(barrier, 4)
    cols = pl.ds(pl.multiple_of(core * chans, chans), chans)
    swap = remote(
        normed_ref.at[pl.ds(pl.multiple_of((1 - core) * half, half), half)],
        whole.at[:, cols], sib_send, sib_recv, sibling,
    )
    swap.start()
    whole[:, cols] = normed_ref[pl.ds(pl.multiple_of(core * half, half), half), :]
    swap.wait_recv()

    inner = m * (3 - m) // 2
    end = inner * 3 * (m - 1) + (1 - inner) * m
    near = 1 + end // 3
    far = 3 - near
    opp = 3 - end

    def block(j):
        return pl.ds(pl.multiple_of(j * part, part), part)

    def hop(i, slot, to, t):
        c = pl.ds(t * step, step)
        return pltpu.make_async_remote_copy(
            src_ref=sent.at[i, :, c], dst_ref=got.at[slot, :, c],
            send_sem=send_sem.at[i, t], recv_sem=recv_sem.at[slot, t],
            device_id={"mp": to}, device_id_type=MESH,
        )

    for t in range(TILES):
        loads[t].wait()

        @pl.loop(0, step // 256)
        def _(u):
            c = pl.ds(pl.multiple_of(t * step + u * 256, 256), 256)
            own[:, c] = lax.dot_general(
                whole[...], wbuf[c, :], (((1,), (1,)), ((), ())),
                preferred_element_type=jnp.float32,
            )

        c = pl.ds(t * step, step)

        @pl.when(inner == 0)
        def _():
            for slot, j in ((2, opp), (1, far), (0, near)):
                sent[slot, :, c] = own[block(j), c].astype(jnp.bfloat16)
                hop(slot, slot, near, t).start()

        @pl.when(inner == 1)
        def _():
            sent[0, :, c] = own[block(end), c].astype(jnp.bfloat16)
            hop(0, 0, end, t).start()

    @pl.when(inner == 1)
    def _():
        for t in range(TILES):
            c = pl.ds(t * step, step)
            for i, slot, j in ((1, 1, opp), (2, 3, far)):
                held = 2 if i == 1 else 1
                hop(i, held, j, t).wait_recv()
                sent[i, :, c] = (
                    own[block(j), c] + got[held, :, c].astype(jnp.float32)
                ).astype(jnp.bfloat16)
                hop(i, slot, j, t).start()
        for t in range(TILES):
            c = pl.ds(t * step, step)
            hop(0, 0, end, t).wait_recv()
            hop(0, 3, end, t).wait_recv()
            out_ref[:, c] = (
                own[block(m), c] + got[0, :, c].astype(jnp.float32)
                + got[3, :, c].astype(jnp.float32)
            ).astype(jnp.bfloat16)

    @pl.when(inner == 0)
    def _():
        for t in range(TILES):
            c = pl.ds(t * step, step)
            hop(0, 0, near, t).wait_recv()
            hop(0, 1, near, t).wait_recv()
            out_ref[:, c] = (
                own[block(m), c] + got[0, :, c].astype(jnp.float32)
                + got[1, :, c].astype(jnp.float32)
            ).astype(jnp.bfloat16)

    for t in range(TILES):
        for i in range(3):
            hop(i, 0, near * (1 - inner) + end * inner, t).wait_send()
    swap.wait_send()


def project_out(normed, w_out):
    half, chans = normed.shape[0] // 2, normed.shape[1]
    feats = w_out.shape[0]
    bf = jnp.bfloat16
    vmem = pl.BlockSpec(memory_space=pltpu.VMEM)
    dma = pltpu.SemaphoreType.DMA
    return pl.pallas_call(
        output_kernel,
        out_shape=jax.ShapeDtypeStruct((half // 4, feats), bf),
        in_specs=[vmem, pl.BlockSpec(memory_space=pl.ANY)],
        out_specs=vmem,
        scratch_shapes=[
            pltpu.VMEM((half, 2 * chans), bf),
            pltpu.VMEM((feats, 2 * chans), bf),
            pltpu.VMEM((half, feats), jnp.float32),
            pltpu.VMEM((3, half // 4, feats), bf),
            pltpu.VMEM((4, half // 4, feats), bf),
            dma((TILES,)), dma, dma, dma((3, TILES)), dma((4, TILES)),
        ],
        compiler_params=pltpu.CompilerParams(
            collective_id=1, has_side_effects=True, vmem_limit_bytes=48 << 20
        ),
    )(normed, w_out)


def on_plane(
    tokens, pack_source, segment_ids, w_in, w_dt, w_out, conv_x, conv_bc,
    dt_bias, decay_rate, skip_gain, norm_gain,
):
    f32, bf = jnp.float32, jnp.bfloat16
    rows = tokens.shape[0]
    total = 8 * rows
    block = 2 * rows
    me = lax.axis_index("dp")
    core, chip = me % 2, me // 2
    heads = w_dt.shape[1] // 2
    chans = w_out.shape[1] // 2

    def mine(values, axis):
        size = values.shape[axis] // 2
        return lax.dynamic_slice_in_dim(values, core * size, size, axis)

    meta = jnp.pad(jnp.stack([pack_source, segment_ids]), ((0, 6), (0, 0)))
    halves = w_dt.reshape(w_dt.shape[0], 2, heads).transpose(1, 0, 2)
    wdt = jnp.pad(jnp.concatenate([halves, halves], axis=2), ((0, 0), (0, 0), (0, 128 - 2 * heads)))
    xb, dt_raw, zc, metas = project(tokens, meta, w_in, wdt)
    seg_all = jnp.concatenate([jnp.full((HALO,), -1, jnp.int32), metas[:, 1, :].reshape(total)])
    seg_ext = lax.dynamic_slice_in_dim(seg_all, chip * block, block + HALO, 0)
    seg = seg_ext[HALO:]
    seg_before = seg_ext[HALO - 1]
    taps_bc = mine(conv_bc, 2)

    def convolve(values, taps):
        total_sum = jnp.zeros((block, values.shape[1]), f32)
        for lag in range(CONV):
            first = HALO - CONV + 1 + lag
            same = (seg_ext[first : first + block] == seg)[:, None]
            total_sum = total_sum + jnp.where(
                same, taps[lag][None, :] * values[first : first + block].astype(f32), 0.0
            )
        return jax.nn.silu(total_sum).astype(bf)

    x = convolve(xb[:, :chans], mine(conv_x, 1))
    b = convolve(xb[:, chans:], taps_bc[:, 0])
    c = convolve(zc[:, chans:], taps_bc[:, 1])
    gate = jax.nn.silu(zc[HALO:, :chans].astype(f32))
    step_dt = jax.nn.softplus(dt_raw[HALO:, :heads] + mine(dt_bias, 0))
    step_rate = -step_dt * mine(decay_rate, 0)
    places = jnp.arange(block)
    lower = (places[:, None] >= places[None, :])
    cum = jnp.dot(lower.astype(f32), step_rate, precision=highest)
    xh = x.reshape(block, heads, HEAD_DIM)

    last = seg[-1]
    weight = jnp.where((seg == last)[:, None], jnp.exp(cum[-1][None, :] - cum), 0.0) * step_dt
    wide = jnp.repeat(weight, HEAD_DIM, axis=1)
    weighted = (wide * x.astype(f32)).astype(bf)
    left = lax.dot_general(weighted, b, (((0,), (0,)), ((), ())), preferred_element_type=f32)
    gain = jnp.where(last == seg_before, jnp.exp(cum[-1]), 0.0)
    sent = jnp.concatenate(
        [left.reshape(heads, HEAD_DIM * STATE), jnp.broadcast_to(gain[:, None], (heads, 128))], axis=1
    ).astype(bf)
    groups = [[i, i + 2, i + 4, i + 6] for i in range(2)]
    gathered = lax.all_gather(sent, "dp", axis_index_groups=groups).astype(f32)

    linked = (seg[:, None] == seg[None, :]) & lower
    cum_t = cum.T
    spans = cum_t[:, :, None] - cum_t[:, None, :]
    decay = jnp.where(linked[None], jnp.exp(jnp.where(linked[None], spans, 0.0)), 0.0)
    scores = lax.dot_general(c, b, (((1,), (1,)), ((), ())), preferred_element_type=f32)
    mixing = (scores[None] * decay * step_dt.T[:, None, :]).astype(bf)
    ssd = jnp.einsum("hts,shp->thp", mixing, xh, preferred_element_type=f32).reshape(block, chans)

    incoming = jnp.zeros((heads, HEAD_DIM * STATE), f32)
    for k in range(3):
        part = gathered[k]
        incoming = jnp.where(
            k < chip, part[:, -1:] * incoming + part[:, : HEAD_DIM * STATE], incoming
        )
    before = incoming.reshape(chans, STATE).astype(bf)
    entry = jnp.where((seg == seg_before)[:, None], jnp.exp(cum), 0.0)
    ssd = ssd + jnp.repeat(entry, HEAD_DIM, axis=1) * lax.dot_general(
        c, before, (((1,), (1,)), ((), ())), preferred_element_type=f32
    )
    skip = jnp.repeat(mine(skip_gain, 0), HEAD_DIM)[None, :]
    gated = (ssd + skip * x.astype(f32)) * gate
    inv = lax.rsqrt(jnp.mean(gated * gated, axis=1, keepdims=True) + 1e-05)
    normed = (gated * inv * mine(norm_gain, 0)[None, :]).astype(bf)

    return project_out(normed, w_out)


def solution(mesh):
    placed = (
        P("dp", None),
        P("dp"),
        P("dp"),
        P("dp", "mp"),
        P("dp", "mp"),
        P(None, "mp"),
        P(None, "mp"),
        P(None, None, "mp"),
        P("mp"),
        P("mp"),
        P("mp"),
        P("mp"),
    )
    body = on_plane if mesh.shape["dp"] == 8 and mesh.shape["mp"] == 4 else on_device
    return jax.shard_map(
        body, mesh=mesh, in_specs=placed, out_specs=P(("dp", "mp"), None), check_vma=False
    )
```

```python
import jax
import jax.numpy as jnp
from jax import lax
from jax.experimental import pallas as pl
from jax.experimental.pallas import tpu as pltpu
from jax.sharding import PartitionSpec as P

HEAD_DIM = 64
STATE = 256
CONV = 4
BLOCK = 256


highest = lax.Precision.HIGHEST


def passed_along(x, axis, by):
    size = lax.axis_size(axis)
    pairs = [(i, i + by) for i in range(size) if 0 <= i + by < size]
    return lax.ppermute(x, axis, pairs)


def carried_in(x, axis, join, neutral):
    place = lax.axis_index(axis)
    gathered = jax.tree.map(
        lambda a, kind: lax.all_gather(a.astype(kind), axis), x, (jnp.bfloat16, jnp.bfloat16)
    )
    state = jax.tree.map(lambda a, e: jnp.zeros_like(a) + jnp.asarray(e, a.dtype), x, neutral)

    def one(hop, state):
        return join(
            state,
            jax.tree.map(
                lambda a, own: lax.dynamic_index_in_dim(a, hop, 0, False).astype(own.dtype),
                gathered,
                x,
            ),
        )

    return lax.fori_loop(0, place, one, state)


def chain_combine(earlier, later_part):
    return (earlier[0] * later_part[0], later_part[0][:, None, None] * earlier[1] + later_part[1])


def block_step(carry, pieces):
    state_now, prev_seg = carry
    x_block, b_block, c_block, step_dt, step_rate, seg_block = pieces
    per_group = x_block.shape[1] // b_block.shape[1]
    cum_rate = jnp.cumsum(step_rate, axis=0)
    places = jnp.arange(seg_block.shape[0])
    linked = (seg_block[:, None] == seg_block[None, :]) & (places[:, None] >= places[None, :])
    log_spans = cum_rate.T[:, :, None] - cum_rate.T[:, None, :]
    decay_mat = jnp.where(linked[None], jnp.exp(jnp.where(linked[None], log_spans, 0.0)), 0.0)
    scores = jnp.einsum("tgn,sgn->gts", c_block, b_block, preferred_element_type=jnp.float32)
    scores = jnp.repeat(scores, per_group, axis=0)
    mixing = (scores * decay_mat * step_dt.T[:, None, :]).astype(jnp.bfloat16)
    in_block = jnp.einsum("hts,shp->thp", mixing, x_block, preferred_element_type=jnp.float32)
    c_heads = jnp.repeat(c_block.astype(jnp.float32), per_group, axis=1)
    b_heads = jnp.repeat(b_block.astype(jnp.float32), per_group, axis=1)
    entry_mask = jnp.where((seg_block == prev_seg)[:, None], jnp.exp(cum_rate), 0.0)
    from_before = entry_mask[:, :, None] * jnp.einsum(
        "thn,hpn->thp", c_heads, state_now, precision=highest
    )
    last_seg = seg_block[-1]
    weight = (
        jnp.where((seg_block == last_seg)[:, None], jnp.exp(cum_rate[-1][None, :] - cum_rate), 0.0)
        * step_dt
    )
    carried = jnp.where(last_seg == prev_seg, jnp.exp(cum_rate[-1]), 0.0)
    added_in = jnp.einsum(
        "shp,shn->hpn", weight[:, :, None] * x_block.astype(jnp.float32), b_heads, precision=highest
    )
    return ((carried[:, None, None] * state_now + added_in, last_seg), in_block + from_before)


def on_device(
    tokens,
    pack_source,
    segment_ids,
    w_in,
    w_dt,
    w_out,
    conv_x,
    conv_bc,
    dt_bias,
    decay_rate,
    skip_gain,
    norm_gain,
):
    row_count = tokens.shape[0]
    data_devs = lax.axis_size("dp")
    capacity = 2 * row_count // data_devs
    source_dev = pack_source // row_count
    source_row = pack_source % row_count
    same_source = source_dev[:, None] == source_dev[None, :]
    earlier_rows = pack_source[None, :] < pack_source[:, None]
    rank_in = jnp.sum((same_source & earlier_rows).astype(jnp.int32), axis=1)
    slot_index = source_dev * capacity + rank_in
    requests = (
        jnp.full((data_devs * capacity,), -1, jnp.int32)
        .at[slot_index]
        .set(source_row)
        .reshape(data_devs, capacity)
    )
    wanted = lax.all_to_all(requests, "dp", split_axis=0, concat_axis=0, tiled=True)
    fetched = jnp.where(
        (wanted >= 0)[:, :, None], tokens[jnp.maximum(wanted, 0)], jnp.zeros((), jnp.bfloat16)
    )
    replies = lax.all_to_all(fetched, "dp", split_axis=0, concat_axis=0, tiled=True)
    gathered = replies.reshape(data_devs * capacity, tokens.shape[1])[slot_index]
    panel_cols = w_in.shape[1]
    head_count = w_dt.shape[1]
    chan_width = w_out.shape[1]
    proj_sum = jnp.dot(
        gathered, lax.all_gather(w_in, "dp", axis=0, tiled=True), preferred_element_type=jnp.float32
    )
    step_sum = jnp.dot(
        gathered, lax.all_gather(w_dt, "dp", axis=0, tiled=True), preferred_element_type=jnp.float32
    )
    proj_sum, dt_raw = (proj_sum, step_sum)
    projected = proj_sum.astype(jnp.bfloat16)
    group_width = (panel_cols - 2 * chan_width) // 2
    gate_in = projected[:, chan_width : 2 * chan_width]
    stacked = jnp.concatenate([projected[:, :chan_width], projected[:, 2 * chan_width :]], axis=1)
    tail_len = CONV - 1
    tail_vals = stacked[row_count - tail_len :].astype(jnp.float32)
    tail_seg = (segment_ids[row_count - tail_len :] + 1).astype(jnp.float32)
    prev_vals, prev_seg = passed_along((tail_vals, tail_seg), "dp", 1)
    extended = jnp.concatenate([prev_vals.astype(jnp.bfloat16), stacked], axis=0)
    seg_ext = jnp.concatenate([prev_seg.astype(jnp.int32) - 1, segment_ids], axis=0)
    kernel = jnp.concatenate([conv_x, conv_bc.reshape(CONV, 2 * group_width)], axis=1)
    conv_sum = jnp.zeros((row_count, stacked.shape[1]), jnp.float32)
    for lag_index in range(CONV):
        same_seg = (seg_ext[lag_index : lag_index + row_count] == segment_ids)[:, None]
        conv_sum = conv_sum + jnp.where(
            same_seg,
            kernel[lag_index][None, :]
            * extended[lag_index : lag_index + row_count].astype(jnp.float32),
            0.0,
        )
    convolved = jax.nn.silu(conv_sum).astype(jnp.bfloat16)
    local_groups = group_width // STATE
    x_all = convolved[:, :chan_width].reshape(row_count, head_count, HEAD_DIM)
    b_all = convolved[:, chan_width : chan_width + group_width].reshape(
        row_count, local_groups, STATE
    )
    c_all = convolved[:, chan_width + group_width :].reshape(row_count, local_groups, STATE)
    step_dt = jax.nn.softplus(dt_raw + dt_bias)
    step_rate = -step_dt * decay_rate
    seg_before = seg_ext[tail_len - 1]
    block_total = row_count // BLOCK

    def to_blocks(values):
        return values.reshape((block_total, BLOCK) + values.shape[1:])

    start_state = (jnp.zeros((head_count, HEAD_DIM, STATE), jnp.float32), seg_before)
    final, outputs = lax.scan(
        block_step,
        start_state,
        (
            to_blocks(x_all),
            to_blocks(b_all),
            to_blocks(c_all),
            to_blocks(step_dt),
            to_blocks(step_rate),
            to_blocks(segment_ids),
        ),
    )
    local_state = final[0]
    scan_out = outputs.reshape(row_count, head_count, HEAD_DIM)
    running = jnp.cumsum(step_rate, axis=0)
    carry_gain = jnp.where(segment_ids[-1] == seg_before, jnp.exp(running[-1]), 0.0)
    neutral = (jnp.ones((head_count,), jnp.float32), jnp.zeros_like(local_state))
    incoming = carried_in((carry_gain, local_state), "dp", chain_combine, neutral)[1]
    c_heads = jnp.repeat(c_all.astype(jnp.float32), head_count // local_groups, axis=1)
    entry_mask = jnp.where((segment_ids == seg_before)[:, None], jnp.exp(running), 0.0)
    scan_out = scan_out + entry_mask[:, :, None] * jnp.einsum(
        "thn,hpn->thp", c_heads, incoming, precision=highest
    )
    scan_out = scan_out + skip_gain[None, :, None] * x_all.astype(jnp.float32)
    gated_out = scan_out.reshape(row_count, chan_width) * jax.nn.silu(gate_in.astype(jnp.float32))
    grouped = gated_out.reshape(row_count, local_groups, chan_width // local_groups)
    inv_rms = lax.rsqrt(jnp.mean(grouped * grouped, axis=2, keepdims=True) + 1e-05)
    normed = ((grouped * inv_rms).reshape(row_count, chan_width) * norm_gain).astype(jnp.bfloat16)
    return lax.psum_scatter(
        lax.dot_general(
            normed, w_out, (((1,), (1,)), ((), ())), preferred_element_type=jnp.float32
        ).astype(jnp.bfloat16),
        "mp",
        scatter_dimension=0,
        tiled=True,
    )


HALO = 16
MESH = pl.DeviceIdType.MESH


def remote(src, dst, send, recv, dp):
    return pltpu.make_async_remote_copy(
        src_ref=src, dst_ref=dst, send_sem=send, recv_sem=recv,
        device_id={"dp": dp}, device_id_type=MESH,
    )


def projection_kernel(
    tok_hbm, meta_ref, w_hbm, wdt_ref,
    xb_out, dt_out, zc_out, meta_out,
    tokg, metas, wbuf, idxcol, onehot, packed, own,
    s_da, s_db, s_xa, s_yb, s_ya, s_xb,
    r_da, r_db, r_xa, r_yb, r_sa, r_sb,
    loc_sem, meta_send, meta_recv, w_send, w_recv,
    tok_send, tok_recv, fwd_send, fwd_recv, red_send, red_recv,
):
    me = lax.axis_index("dp")
    core = me % 2
    chip = me // 2
    at_x = chip % 2
    at_y = chip // 2
    chip_x = chip + 1 - 2 * at_x
    chip_y = chip + 2 - 4 * at_y
    chip_d = chip_x + chip_y - chip
    sibling = me + 1 - 2 * core
    rows, depth = tok_hbm.shape[0], w_hbm.shape[0]
    width = w_hbm.shape[1] // 5
    group, state = width, width // 4
    kdim = 2 * depth
    block = 2 * rows
    na = xb_out.shape[1]
    nb = zc_out.shape[1]

    barrier = pltpu.get_barrier_semaphore()
    for k in range(1, 8):
        pl.semaphore_signal(barrier, inc=1, device_id={"dp": (me + k) % 8}, device_id_type=MESH)
    pl.semaphore_wait(barrier, 7)

    mine = pl.ds(pl.multiple_of(me * rows, rows), rows)

    def columns(of_chip):
        return pl.ds(pl.multiple_of(of_chip * kdim, 128), kdim)

    copies = []
    for k in range(1, 8):
        copies.append(
            remote(meta_ref, metas.at[me], meta_send.at[k - 1], meta_recv.at[k - 1], (me + k) % 8)
        )
    directs = []
    for i, to in enumerate((chip_d, chip_x, chip_y)):
        directs.append(
            remote(tok_hbm.at[:, columns(to)], tokg.at[mine], tok_send.at[i], tok_recv.at[i],
                   2 * to + core)
        )
    for c in copies + directs:
        c.start()
    local = [
        pltpu.make_async_copy(tok_hbm.at[:, columns(chip)], tokg.at[mine], loc_sem.at[0]),
        pltpu.make_async_copy(meta_ref, metas.at[me], loc_sem.at[1]),
    ]
    forward = [
        remote(tok_hbm.at[:, columns(chip)], tokg.at[mine], fwd_send.at[0], fwd_recv.at[0], sibling)
    ]
    kmine = pl.ds(pl.multiple_of(core * depth, depth), depth)

    def pieces(g):
        return (
            (w_hbm.at[:, pl.ds(pl.multiple_of(g * group, 128), group)], 0, group),
            (w_hbm.at[:, pl.ds(pl.multiple_of(4 * group + g * state, 128), state)], group, state),
            (wdt_ref.at[g], na, 128),
            (w_hbm.at[:, pl.ds(pl.multiple_of(2 * group + g * group, 128), group)], na + 128, group),
            (w_hbm.at[:, pl.ds(pl.multiple_of(4 * group + 2 * state + g * state, 128), state)],
             na + 128 + group, state),
        )

    weights = []
    for i, (src, col, size) in enumerate(pieces(1 - core)):
        weights.append(
            remote(src, wbuf.at[kmine, pl.ds(col, size)], w_send.at[i], w_recv.at[i], sibling)
        )
    for i, (src, col, size) in enumerate(pieces(core)):
        local.append(
            pltpu.make_async_copy(src, wbuf.at[kmine, pl.ds(col, size)], loc_sem.at[2 + i])
        )
    for c in forward + weights + local:
        c.start()

    for c in copies:
        c.wait_recv()
    local[1].wait()
    idxcol[0:HALO, :] = jnp.full((HALO, 128), -1, jnp.int32)
    for j in range(8):
        row = metas[j, 0:1, :]
        idxcol[HALO + j * rows : HALO + (j + 1) * rows, :] = jnp.broadcast_to(row, (128, rows)).T
    meta_out[...] = metas[...]

    for i, source in enumerate((chip_d, chip_x, chip_y)):
        directs[i].wait_recv()
        theirs = pl.ds(pl.multiple_of((2 * source + core) * rows, rows), rows)
        c = remote(tokg.at[theirs], tokg.at[theirs], fwd_send.at[1 + i], fwd_recv.at[1 + i], sibling)
        c.start()
        forward.append(c)
    for c in local[:1] + local[2:]:
        c.wait()
    for c in weights + forward:
        c.wait_recv()

    lanes = lax.broadcasted_iota(jnp.int32, (block + HALO, 128), 1)

    def pack(of_chip, slot):
        ids = idxcol[pl.ds(pl.multiple_of(of_chip * block, block), block + HALO), :]

        @pl.loop(0, 8 * rows // 128)
        def _(t):
            onehot[:, pl.ds(pl.multiple_of(t * 128, 128), 128)] = jnp.where(
                ids == lanes + t * 128, 1.0, 0.0
            ).astype(jnp.bfloat16)

        @pl.loop(0, kdim // 256)
        def _(t):
            cols = pl.ds(pl.multiple_of(t * 256, 256), 256)
            packed[slot, :, cols] = jnp.dot(
                onehot[...], tokg[:, cols], preferred_element_type=jnp.float32
            ).astype(jnp.bfloat16)

    def product(slot, col, size):
        return jnp.dot(
            packed[slot], wbuf[:, pl.ds(col, size)], preferred_element_type=jnp.float32
        )

    def split(acc):
        high = acc.astype(jnp.bfloat16).astype(jnp.float32)
        return jnp.where(lanes < 16, high, acc - high).astype(jnp.bfloat16)

    def joined(ref):
        r = ref[:, na : na + 128].astype(jnp.float32)
        return r + jnp.where(lanes < 16, pltpu.roll(r, 112, 1), pltpu.roll(r, 16, 1))

    def part_a(slot, out, add=None):
        @pl.loop(0, na // 256)
        def _(t):
            col = pl.multiple_of(t * 256, 256)
            acc = product(slot, col, 256)
            if add is not None:
                acc = acc + add[:, pl.ds(col, 256)].astype(jnp.float32)
            out[:, pl.ds(col, 256)] = acc.astype(jnp.bfloat16)

        acc = product(slot, na, 128)
        if add is not None:
            acc = acc + joined(add)
        out[:, na : na + 128] = split(acc)

    def part_b(slot, out, add=None):
        @pl.loop(0, nb // 256)
        def _(t):
            col = pl.multiple_of(t * 256, 256)
            acc = product(slot, pl.multiple_of(na + 128 + col, 128), 256)
            if add is not None:
                acc = acc + add[:, pl.ds(col, 256)].astype(jnp.float32)
            out[:, pl.ds(col, 256)] = acc.astype(jnp.bfloat16)

    dev_x, dev_y = 2 * chip_x + core, 2 * chip_y + core
    c_da = remote(s_da, r_da, red_send.at[0], red_recv.at[0], dev_x)
    c_db = remote(s_db, r_db, red_send.at[1], red_recv.at[1], dev_y)
    c_xa = remote(s_xa, r_xa, red_send.at[2], red_recv.at[2], dev_x)
    c_yb = remote(s_yb, r_yb, red_send.at[3], red_recv.at[3], dev_y)
    c_ya = remote(s_ya, r_sa, red_send.at[4], red_recv.at[4], dev_y)
    c_xb = remote(s_xb, r_sb, red_send.at[5], red_recv.at[5], dev_x)
    pack(chip_d, 0)
    part_a(0, s_da)
    c_da.start()
    part_b(0, s_db)
    c_db.start()
    pack(chip_x, 1)
    part_a(1, s_xa)
    c_xa.start()
    pack(chip_y, 2)
    part_b(2, s_yb)
    c_yb.start()
    pack(chip, 0)

    @pl.loop(0, na // 256)
    def _(t):
        col = pl.multiple_of(t * 256, 256)
        own[:, pl.ds(col, 256)] = product(0, col, 256)

    own[:, na : na + 128] = product(0, na, 128)

    @pl.loop(0, nb // 256)
    def _(t):
        col = pl.multiple_of(na + 128 + t * 256, 128)
        own[:, pl.ds(col, 256)] = product(0, col, 256)

    c_da.wait_recv()
    part_a(2, s_ya, r_da)
    c_ya.start()
    c_db.wait_recv()
    part_b(1, s_xb, r_db)
    c_xb.start()
    c_xa.wait_recv()
    c_yb.wait_recv()
    c_ya.wait_recv()

    @pl.loop(0, na // 256)
    def _(t):
        cols = pl.ds(pl.multiple_of(t * 256, 256), 256)
        xb_out[:, cols] = (
            own[:, cols] + r_xa[:, cols].astype(jnp.float32) + r_sa[:, cols].astype(jnp.float32)
        ).astype(jnp.bfloat16)

    dt_out[...] = own[:, na : na + 128] + joined(r_xa) + joined(r_sa)
    c_xb.wait_recv()

    @pl.loop(0, nb // 256)
    def _(t):
        cols = pl.ds(pl.multiple_of(t * 256, 256), 256)
        own_cols = pl.ds(pl.multiple_of(na + 128 + t * 256, 128), 256)
        zc_out[:, cols] = (
            own[:, own_cols] + r_yb[:, cols].astype(jnp.float32) + r_sb[:, cols].astype(jnp.float32)
        ).astype(jnp.bfloat16)

    for c in copies + directs + forward + weights + [c_da, c_db, c_xa, c_yb, c_ya, c_xb]:
        c.wait_send()


def project(tokens, meta, w_in, wdt):
    rows, depth = tokens.shape[0], w_in.shape[0]
    width = w_in.shape[1] // 5
    na = width + width // 4
    nb = na
    m = 2 * rows + HALO
    bf = jnp.bfloat16
    vmem = pl.BlockSpec(memory_space=pltpu.VMEM)
    hbm = pl.BlockSpec(memory_space=pl.ANY)
    dma = pltpu.SemaphoreType.DMA
    a, b = pltpu.VMEM((m, na + 128), bf), pltpu.VMEM((m, nb), bf)
    return pl.pallas_call(
        projection_kernel,
        out_shape=(
            jax.ShapeDtypeStruct((m, na), bf),
            jax.ShapeDtypeStruct((m, 128), jnp.float32),
            jax.ShapeDtypeStruct((m, nb), bf),
            jax.ShapeDtypeStruct((8, 8, rows), jnp.int32),
        ),
        in_specs=[hbm, vmem, hbm, vmem],
        out_specs=(vmem,) * 4,
        scratch_shapes=[
            pltpu.VMEM((8 * rows, 2 * depth), bf),
            pltpu.VMEM((8, 8, rows), jnp.int32),
            pltpu.VMEM((2 * depth, na + 128 + nb), bf),
            pltpu.VMEM((8 * rows + HALO, 128), jnp.int32),
            pltpu.VMEM((m, 8 * rows), bf),
            pltpu.VMEM((3, m, 2 * depth), bf),
            pltpu.VMEM((m, na + 128 + nb), jnp.float32),
            a, b, a, b, a, b,
            a, b, a, b, a, b,
            dma((7,)), dma((7,)), dma((7,)), dma((5,)), dma((5,)),
            dma((3,)), dma((3,)), dma((4,)), dma((4,)), dma((6,)), dma((6,)),
        ],
        compiler_params=pltpu.CompilerParams(
            collective_id=0, has_side_effects=True, vmem_limit_bytes=58 << 20
        ),
    )(tokens, meta, w_in, wdt)


TILES = 4


def output_kernel(normed_ref, w_hbm, out_ref, whole, wbuf, own, sent, got,
                  loc_sem, sib_send, sib_recv, send_sem, recv_sem):
    dp, m = lax.axis_index("dp"), lax.axis_index("mp")
    core = dp % 2
    sibling = dp + 1 - 2 * core
    half = normed_ref.shape[0] // 2
    chans = normed_ref.shape[1]
    part = half // 4
    step = w_hbm.shape[0] // TILES

    barrier = pltpu.get_barrier_semaphore()
    pl.semaphore_signal(barrier, inc=1, device_id={"dp": sibling}, device_id_type=MESH)
    for k in range(1, 4):
        pl.semaphore_signal(barrier, inc=1, device_id={"mp": (m + k) % 4}, device_id_type=MESH)
    loads = []
    for t in range(TILES):
        rows = pl.ds(t * step, step)
        loads.append(pltpu.make_async_copy(w_hbm.at[rows], wbuf.at[rows], loc_sem.at[t]))
        loads[t].start()
    pl.semaphore_wait(barrier, 4)
    cols = pl.ds(pl.multiple_of(core * chans, chans), chans)
    swap = remote(
        normed_ref.at[pl.ds(pl.multiple_of((1 - core) * half, half), half)],
        whole.at[:, cols], sib_send, sib_recv, sibling,
    )
    swap.start()
    whole[:, cols] = normed_ref[pl.ds(pl.multiple_of(core * half, half), half), :]
    swap.wait_recv()

    inner = m * (3 - m) // 2
    end = inner * 3 * (m - 1) + (1 - inner) * m
    near = 1 + end // 3
    far = 3 - near
    opp = 3 - end

    def block(j):
        return pl.ds(pl.multiple_of(j * part, part), part)

    def hop(i, slot, to, t):
        c = pl.ds(t * step, step)
        return pltpu.make_async_remote_copy(
            src_ref=sent.at[i, :, c], dst_ref=got.at[slot, :, c],
            send_sem=send_sem.at[i, t], recv_sem=recv_sem.at[slot, t],
            device_id={"mp": to}, device_id_type=MESH,
        )

    for t in range(TILES):
        loads[t].wait()

        @pl.loop(0, step // 256)
        def _(u):
            c = pl.ds(pl.multiple_of(t * step + u * 256, 256), 256)
            own[:, c] = lax.dot_general(
                whole[...], wbuf[c, :], (((1,), (1,)), ((), ())),
                preferred_element_type=jnp.float32,
            )

        c = pl.ds(t * step, step)

        @pl.when(inner == 0)
        def _():
            for slot, j in ((2, opp), (1, far), (0, near)):
                sent[slot, :, c] = own[block(j), c].astype(jnp.bfloat16)
                hop(slot, slot, near, t).start()

        @pl.when(inner == 1)
        def _():
            sent[0, :, c] = own[block(end), c].astype(jnp.bfloat16)
            hop(0, 0, end, t).start()

    @pl.when(inner == 1)
    def _():
        for t in range(TILES):
            c = pl.ds(t * step, step)
            for i, slot, j in ((1, 1, opp), (2, 3, far)):
                held = 2 if i == 1 else 1
                hop(i, held, j, t).wait_recv()
                sent[i, :, c] = (
                    own[block(j), c] + got[held, :, c].astype(jnp.float32)
                ).astype(jnp.bfloat16)
                hop(i, slot, j, t).start()
        for t in range(TILES):
            c = pl.ds(t * step, step)
            hop(0, 0, end, t).wait_recv()
            hop(0, 3, end, t).wait_recv()
            out_ref[:, c] = (
                own[block(m), c] + got[0, :, c].astype(jnp.float32)
                + got[3, :, c].astype(jnp.float32)
            ).astype(jnp.bfloat16)

    @pl.when(inner == 0)
    def _():
        for t in range(TILES):
            c = pl.ds(t * step, step)
            hop(0, 0, near, t).wait_recv()
            hop(0, 1, near, t).wait_recv()
            out_ref[:, c] = (
                own[block(m), c] + got[0, :, c].astype(jnp.float32)
                + got[1, :, c].astype(jnp.float32)
            ).astype(jnp.bfloat16)

    for t in range(TILES):
        for i in range(3):
            hop(i, 0, near * (1 - inner) + end * inner, t).wait_send()
    swap.wait_send()


def project_out(normed, w_out):
    half, chans = normed.shape[0] // 2, normed.shape[1]
    feats = w_out.shape[0]
    bf = jnp.bfloat16
    vmem = pl.BlockSpec(memory_space=pltpu.VMEM)
    dma = pltpu.SemaphoreType.DMA
    return pl.pallas_call(
        output_kernel,
        out_shape=jax.ShapeDtypeStruct((half // 4, feats), bf),
        in_specs=[vmem, pl.BlockSpec(memory_space=pl.ANY)],
        out_specs=vmem,
        scratch_shapes=[
            pltpu.VMEM((half, 2 * chans), bf),
            pltpu.VMEM((feats, 2 * chans), bf),
            pltpu.VMEM((half, feats), jnp.float32),
            pltpu.VMEM((3, half // 4, feats), bf),
            pltpu.VMEM((4, half // 4, feats), bf),
            dma((TILES,)), dma, dma, dma((3, TILES)), dma((4, TILES)),
        ],
        compiler_params=pltpu.CompilerParams(
            collective_id=1, has_side_effects=True, vmem_limit_bytes=48 << 20
        ),
    )(normed, w_out)


def scan_kernel(
    xb_ref, dt_ref, zc_ref, metas, tapx_ref, tapbc_ref, head_ref, chan_ref,
    normed_ref,
    xs, bs, cs, bt, cum_t, dt_t, w_t, bias, scores, ssd, gz, entry, square, state, got, inc,
    send_sem, recv_sem,
):
    f32, bf = jnp.float32, jnp.bfloat16
    me = lax.axis_index("dp")
    core, chip = me % 2, me // 2
    block, chans = normed_ref.shape
    rows = block // 2
    wide = bs.shape[1]

    barrier = pltpu.get_barrier_semaphore()
    for k in range(1, 4):
        pl.semaphore_signal(
            barrier, inc=1, device_id={"dp": (me + 2 * k) % 8}, device_id_type=MESH
        )
    pl.semaphore_wait(barrier, 3)

    first, second = metas[2 * chip, 1:2, :], metas[2 * chip + 1, 1:2, :]
    earlier = metas[(2 * chip + 7) % 8, 1:2, :]
    follows = (chip + 3) // 4
    earlier = earlier * follows - (1 - follows)

    def column(row):
        return jnp.broadcast_to(row, (128, row.shape[1])).T

    seg_ext = jnp.concatenate(
        [column(earlier)[rows - HALO :], column(first), column(second)], axis=0
    )
    seg_row = jnp.concatenate([first, second], axis=1)
    seg_col = seg_ext[HALO:]
    seg_before = seg_ext[HALO - 1 : HALO]
    seg_last = seg_ext[block + HALO - 1 :]
    same = [jnp.where(pltpu.roll(seg_ext, k, 0) == seg_ext, 1.0, 0.0) for k in range(1, CONV)]

    def convolved(src, col, taps):
        v = src[:, pl.ds(col, 128)].astype(f32)
        total = taps[CONV - 1 : CONV] * v
        for k in range(1, CONV):
            total = total + same[k - 1] * (taps[CONV - 1 - k : CONV - k] * pltpu.roll(v, k, 0))
        total = total[HALO:]
        return (total / (1.0 + jnp.exp(-total))).astype(bf)

    @pl.loop(0, chans // 128)
    def _(t):
        col = pl.multiple_of(t * 128, 128)
        xs[:, pl.ds(col, 128)] = convolved(
            xb_ref, col, tapx_ref[:, pl.ds(pl.multiple_of(core * chans + col, 128), 128)]
        )

    for t in range(wide // 128):
        at = pl.ds(pl.multiple_of(core * wide + t * 128, 128), 128)
        here = pl.ds(t * 128, 128)
        bs[:, here] = convolved(xb_ref, chans + t * 128, tapbc_ref[0, :, at])
        cs[:, here] = convolved(zc_ref, chans + t * 128, tapbc_ref[1, :, at])
    bt[...] = bs[...].astype(f32).T.astype(bf)

    heads = head_ref[core]
    u = dt_ref[HALO:, :] + heads[0:1]
    step_dt = jnp.maximum(u, 0.0) + jnp.log1p(jnp.exp(-jnp.abs(u)))
    rate = -step_dt * heads[1:2]
    lower = jnp.where(
        lax.broadcasted_iota(jnp.int32, (block, block), 0)
        >= lax.broadcasted_iota(jnp.int32, (block, block), 1), 1.0, 0.0
    ).astype(bf)
    high = rate.astype(bf)
    middle = (rate - high.astype(f32)).astype(bf)
    low = (rate - high.astype(f32) - middle.astype(f32)).astype(bf)
    cum = (
        jnp.dot(lower, high, preferred_element_type=f32)
        + jnp.dot(lower, middle, preferred_element_type=f32)
        + jnp.dot(lower, low, preferred_element_type=f32)
    )
    cum_t[...] = cum.T
    dt_t[...] = step_dt.T
    at_last = jnp.where(seg_row == seg_row[:, block - 1 :], 1.0, 0.0)
    w_t[...] = jnp.exp(cum_t[:, block - 1 :] - cum_t[...]) * dt_t[...] * at_last
    enters = jnp.where(seg_col == seg_before, 1.0, 0.0)
    keeps = jnp.where(seg_last == seg_before, 1.0, 0.0)

    def pair_rows(ref, p):
        return ref[pl.ds(2 * p, 1), :], ref[pl.ds(2 * p + 1, 1), :]

    def pair_column(ref, p):
        a, b = pair_rows(ref, p)
        return jnp.concatenate(
            [jnp.broadcast_to(a, (64, block)), jnp.broadcast_to(b, (64, block))], axis=0
        ).T

    @pl.loop(0, chans // 128)
    def _(p):
        cols = pl.ds(pl.multiple_of(p * 128, 128), 128)
        weighted = (pair_column(w_t, p) * xs[:, cols].astype(f32)).astype(bf)
        state[0:wide, cols] = jnp.dot(
            bt[...], weighted, preferred_element_type=f32
        ).astype(bf)
        reach = jnp.exp(pair_column(cum_t, p))
        gain = jnp.broadcast_to(reach[block - 1 :] * keeps, (8, 128))
        rounded = gain.astype(bf).astype(f32)
        state[wide : wide + 16, cols] = jnp.concatenate([rounded, gain - rounded], axis=0).astype(bf)
        entry[:, cols] = reach * enters

    def leave(to):
        return remote(
            state, got.at[chip % 3], send_sem.at[to - 1], recv_sem.at[chip % 3], 2 * to + core
        )

    for to in (3, 2, 1):

        @pl.when(chip < to)
        def _():
            leave(to).start()

    scores[...] = jnp.dot(cs[...], bt[...], preferred_element_type=f32)
    for t in range(block // 128):
        here = slice(t * 128, (t + 1) * 128)
        linked = (seg_col == seg_row[:, here]) & (
            lax.broadcasted_iota(jnp.int32, (block, 128), 0)
            >= lax.broadcasted_iota(jnp.int32, (block, 128), 1) + t * 128
        )
        bias[:, here] = jnp.where(linked, 0.0, -1e30)

    lanes = lax.broadcasted_iota(jnp.int32, (rows, 128), 1)

    @pl.loop(0, chans // 128)
    def _(p):
        cols = pl.ds(pl.multiple_of(p * 128, 128), 128)
        at = pl.ds(pl.multiple_of(core * chans + p * 128, 128), 128)
        cum_rows, dt_rows = pair_rows(cum_t, p), pair_rows(dt_t, p)
        cum_cols = [column(r) for r in cum_rows]
        for i in range(2):
            here = slice(i * rows, (i + 1) * rows)
            w = (i + 1) * rows
            outs = []
            for n in range(2):
                spans = jnp.concatenate([cum_cols[n][here]] * (w // 128), axis=1)
                spans = spans - cum_rows[n][:, :w] + bias[here, :w]
                mixing = (scores[here, :w] * jnp.exp(spans) * dt_rows[n][:, :w]).astype(bf)
                outs.append(jnp.dot(mixing, xs[0:w, cols], preferred_element_type=f32))
            ssd[here, cols] = jnp.where(lanes < 64, outs[0], outs[1]) + chan_ref[
                0:1, at
            ] * xs[here, cols].astype(f32)
        z = zc_ref[:, cols].astype(f32)[HALO:]
        gz[:, cols] = z / (1.0 + jnp.exp(-z))

    inc[...] = jnp.zeros_like(inc)
    for source in range(3):

        @pl.when(source < chip)
        def _():
            remote(
                state, got.at[source], send_sem.at[0], recv_sem.at[source], (me + 2) % 8
            ).wait_recv()
            gain = (
                got[source, wide : wide + 8, :].astype(f32)
                + got[source, wide + 8 : wide + 16, :].astype(f32)
            )[0:1]
            inc[...] = gain * inc[...] + got[source, 0:wide, :].astype(f32)

    square[...] = jnp.zeros_like(square)

    @pl.loop(0, chans // 128)
    def _(p):
        cols = pl.ds(pl.multiple_of(p * 128, 128), 128)
        before = jnp.dot(cs[...], inc[:, cols].astype(bf), preferred_element_type=f32)
        gated = (ssd[:, cols] + entry[:, cols] * before) * gz[:, cols]
        ssd[:, cols] = gated
        square[...] += gated * gated

    inv = lax.rsqrt(jnp.sum(square[...], axis=1, keepdims=True) * (1.0 / chans) + 1e-05)
    inv = jnp.broadcast_to(inv, (block, 128))

    @pl.loop(0, chans // 128)
    def _(p):
        cols = pl.ds(pl.multiple_of(p * 128, 128), 128)
        at = pl.ds(pl.multiple_of(core * chans + p * 128, 128), 128)
        normed_ref[:, cols] = (ssd[:, cols] * inv * chan_ref[1:2, at]).astype(bf)

    for to in (3, 2, 1):

        @pl.when(chip < to)
        def _():
            leave(to).wait_send()


def scan(xb, dt_raw, zc, metas, conv_x, conv_bc, heads, chan):
    f32, bf = jnp.float32, jnp.bfloat16
    block = xb.shape[0] - HALO
    chans = conv_x.shape[1] // 2
    wide = xb.shape[1] - chans
    dma = pltpu.SemaphoreType.DMA
    vmem = pl.BlockSpec(memory_space=pltpu.VMEM)

    def buf(shape, kind=f32):
        return pltpu.VMEM(shape, kind)

    return pl.pallas_call(
        scan_kernel,
        out_shape=jax.ShapeDtypeStruct((block, chans), bf),
        in_specs=[vmem] * 8,
        out_specs=vmem,
        scratch_shapes=[
            buf((block, chans), bf), buf((block, wide), bf), buf((block, wide), bf),
            buf((wide, block), bf),
            buf((128, block)), buf((128, block)), buf((128, block)),
            buf((block, block)), buf((block, block)),
            buf((block, chans)), buf((block, chans)), buf((block, chans)), buf((block, 128)),
            buf((wide + 16, chans), bf), buf((3, wide + 16, chans), bf), buf((wide, chans)),
            dma((3,)), dma((3,)),
        ],
        compiler_params=pltpu.CompilerParams(
            collective_id=2, has_side_effects=True, vmem_limit_bytes=40 << 20
        ),
    )(xb, dt_raw, zc, metas, conv_x, conv_bc, heads, chan)


def on_plane(
    tokens, pack_source, segment_ids, w_in, w_dt, w_out, conv_x, conv_bc,
    dt_bias, decay_rate, skip_gain, norm_gain,
):
    heads = w_dt.shape[1] // 2
    meta = jnp.pad(jnp.stack([pack_source, segment_ids]), ((0, 6), (0, 0)))
    halves = w_dt.reshape(w_dt.shape[0], 2, heads).transpose(1, 0, 2)
    wdt = jnp.pad(jnp.concatenate([halves, halves], axis=2), ((0, 0), (0, 0), (0, 128 - 2 * heads)))
    xb, dt_raw, zc, metas = project(tokens, meta, w_in, wdt)
    params = jnp.stack([dt_bias, decay_rate]).reshape(2, 2, heads).transpose(1, 0, 2)
    params = jnp.pad(params, ((0, 0), (0, 6), (0, 128 - heads)))
    chan = jnp.stack([jnp.repeat(skip_gain, HEAD_DIM), norm_gain])
    normed = scan(xb, dt_raw, zc, metas, conv_x, conv_bc.transpose(1, 0, 2), params, chan)
    return project_out(normed, w_out)


def solution(mesh):
    placed = (
        P("dp", None),
        P("dp"),
        P("dp"),
        P("dp", "mp"),
        P("dp", "mp"),
        P(None, "mp"),
        P(None, "mp"),
        P(None, None, "mp"),
        P("mp"),
        P("mp"),
        P("mp"),
        P("mp"),
    )
    body = on_plane if mesh.shape["dp"] == 8 and mesh.shape["mp"] == 4 else on_device
    return jax.shard_map(
        body, mesh=mesh, in_specs=placed, out_specs=P(("dp", "mp"), None), check_vma=False
    )
```

```python
import jax
import jax.numpy as jnp
from jax import lax
from jax.experimental import pallas as pl
from jax.experimental.pallas import tpu as pltpu
from jax.sharding import PartitionSpec as P

HEAD_DIM = 64
STATE = 256
CONV = 4
BLOCK = 256


highest = lax.Precision.HIGHEST


def passed_along(x, axis, by):
    size = lax.axis_size(axis)
    pairs = [(i, i + by) for i in range(size) if 0 <= i + by < size]
    return lax.ppermute(x, axis, pairs)


def carried_in(x, axis, join, neutral):
    place = lax.axis_index(axis)
    gathered = jax.tree.map(
        lambda a, kind: lax.all_gather(a.astype(kind), axis), x, (jnp.bfloat16, jnp.bfloat16)
    )
    state = jax.tree.map(lambda a, e: jnp.zeros_like(a) + jnp.asarray(e, a.dtype), x, neutral)

    def one(hop, state):
        return join(
            state,
            jax.tree.map(
                lambda a, own: lax.dynamic_index_in_dim(a, hop, 0, False).astype(own.dtype),
                gathered,
                x,
            ),
        )

    return lax.fori_loop(0, place, one, state)


def chain_combine(earlier, later_part):
    return (earlier[0] * later_part[0], later_part[0][:, None, None] * earlier[1] + later_part[1])


def block_step(carry, pieces):
    state_now, prev_seg = carry
    x_block, b_block, c_block, step_dt, step_rate, seg_block = pieces
    per_group = x_block.shape[1] // b_block.shape[1]
    cum_rate = jnp.cumsum(step_rate, axis=0)
    places = jnp.arange(seg_block.shape[0])
    linked = (seg_block[:, None] == seg_block[None, :]) & (places[:, None] >= places[None, :])
    log_spans = cum_rate.T[:, :, None] - cum_rate.T[:, None, :]
    decay_mat = jnp.where(linked[None], jnp.exp(jnp.where(linked[None], log_spans, 0.0)), 0.0)
    scores = jnp.einsum("tgn,sgn->gts", c_block, b_block, preferred_element_type=jnp.float32)
    scores = jnp.repeat(scores, per_group, axis=0)
    mixing = (scores * decay_mat * step_dt.T[:, None, :]).astype(jnp.bfloat16)
    in_block = jnp.einsum("hts,shp->thp", mixing, x_block, preferred_element_type=jnp.float32)
    c_heads = jnp.repeat(c_block.astype(jnp.float32), per_group, axis=1)
    b_heads = jnp.repeat(b_block.astype(jnp.float32), per_group, axis=1)
    entry_mask = jnp.where((seg_block == prev_seg)[:, None], jnp.exp(cum_rate), 0.0)
    from_before = entry_mask[:, :, None] * jnp.einsum(
        "thn,hpn->thp", c_heads, state_now, precision=highest
    )
    last_seg = seg_block[-1]
    weight = (
        jnp.where((seg_block == last_seg)[:, None], jnp.exp(cum_rate[-1][None, :] - cum_rate), 0.0)
        * step_dt
    )
    carried = jnp.where(last_seg == prev_seg, jnp.exp(cum_rate[-1]), 0.0)
    added_in = jnp.einsum(
        "shp,shn->hpn", weight[:, :, None] * x_block.astype(jnp.float32), b_heads, precision=highest
    )
    return ((carried[:, None, None] * state_now + added_in, last_seg), in_block + from_before)


def on_device(
    tokens,
    pack_source,
    segment_ids,
    w_in,
    w_dt,
    w_out,
    conv_x,
    conv_bc,
    dt_bias,
    decay_rate,
    skip_gain,
    norm_gain,
):
    row_count = tokens.shape[0]
    data_devs = lax.axis_size("dp")
    capacity = 2 * row_count // data_devs
    source_dev = pack_source // row_count
    source_row = pack_source % row_count
    same_source = source_dev[:, None] == source_dev[None, :]
    earlier_rows = pack_source[None, :] < pack_source[:, None]
    rank_in = jnp.sum((same_source & earlier_rows).astype(jnp.int32), axis=1)
    slot_index = source_dev * capacity + rank_in
    requests = (
        jnp.full((data_devs * capacity,), -1, jnp.int32)
        .at[slot_index]
        .set(source_row)
        .reshape(data_devs, capacity)
    )
    wanted = lax.all_to_all(requests, "dp", split_axis=0, concat_axis=0, tiled=True)
    fetched = jnp.where(
        (wanted >= 0)[:, :, None], tokens[jnp.maximum(wanted, 0)], jnp.zeros((), jnp.bfloat16)
    )
    replies = lax.all_to_all(fetched, "dp", split_axis=0, concat_axis=0, tiled=True)
    gathered = replies.reshape(data_devs * capacity, tokens.shape[1])[slot_index]
    panel_cols = w_in.shape[1]
    head_count = w_dt.shape[1]
    chan_width = w_out.shape[1]
    proj_sum = jnp.dot(
        gathered, lax.all_gather(w_in, "dp", axis=0, tiled=True), preferred_element_type=jnp.float32
    )
    step_sum = jnp.dot(
        gathered, lax.all_gather(w_dt, "dp", axis=0, tiled=True), preferred_element_type=jnp.float32
    )
    proj_sum, dt_raw = (proj_sum, step_sum)
    projected = proj_sum.astype(jnp.bfloat16)
    group_width = (panel_cols - 2 * chan_width) // 2
    gate_in = projected[:, chan_width : 2 * chan_width]
    stacked = jnp.concatenate([projected[:, :chan_width], projected[:, 2 * chan_width :]], axis=1)
    tail_len = CONV - 1
    tail_vals = stacked[row_count - tail_len :].astype(jnp.float32)
    tail_seg = (segment_ids[row_count - tail_len :] + 1).astype(jnp.float32)
    prev_vals, prev_seg = passed_along((tail_vals, tail_seg), "dp", 1)
    extended = jnp.concatenate([prev_vals.astype(jnp.bfloat16), stacked], axis=0)
    seg_ext = jnp.concatenate([prev_seg.astype(jnp.int32) - 1, segment_ids], axis=0)
    kernel = jnp.concatenate([conv_x, conv_bc.reshape(CONV, 2 * group_width)], axis=1)
    conv_sum = jnp.zeros((row_count, stacked.shape[1]), jnp.float32)
    for lag_index in range(CONV):
        same_seg = (seg_ext[lag_index : lag_index + row_count] == segment_ids)[:, None]
        conv_sum = conv_sum + jnp.where(
            same_seg,
            kernel[lag_index][None, :]
            * extended[lag_index : lag_index + row_count].astype(jnp.float32),
            0.0,
        )
    convolved = jax.nn.silu(conv_sum).astype(jnp.bfloat16)
    local_groups = group_width // STATE
    x_all = convolved[:, :chan_width].reshape(row_count, head_count, HEAD_DIM)
    b_all = convolved[:, chan_width : chan_width + group_width].reshape(
        row_count, local_groups, STATE
    )
    c_all = convolved[:, chan_width + group_width :].reshape(row_count, local_groups, STATE)
    step_dt = jax.nn.softplus(dt_raw + dt_bias)
    step_rate = -step_dt * decay_rate
    seg_before = seg_ext[tail_len - 1]
    block_total = row_count // BLOCK

    def to_blocks(values):
        return values.reshape((block_total, BLOCK) + values.shape[1:])

    start_state = (jnp.zeros((head_count, HEAD_DIM, STATE), jnp.float32), seg_before)
    final, outputs = lax.scan(
        block_step,
        start_state,
        (
            to_blocks(x_all),
            to_blocks(b_all),
            to_blocks(c_all),
            to_blocks(step_dt),
            to_blocks(step_rate),
            to_blocks(segment_ids),
        ),
    )
    local_state = final[0]
    scan_out = outputs.reshape(row_count, head_count, HEAD_DIM)
    running = jnp.cumsum(step_rate, axis=0)
    carry_gain = jnp.where(segment_ids[-1] == seg_before, jnp.exp(running[-1]), 0.0)
    neutral = (jnp.ones((head_count,), jnp.float32), jnp.zeros_like(local_state))
    incoming = carried_in((carry_gain, local_state), "dp", chain_combine, neutral)[1]
    c_heads = jnp.repeat(c_all.astype(jnp.float32), head_count // local_groups, axis=1)
    entry_mask = jnp.where((segment_ids == seg_before)[:, None], jnp.exp(running), 0.0)
    scan_out = scan_out + entry_mask[:, :, None] * jnp.einsum(
        "thn,hpn->thp", c_heads, incoming, precision=highest
    )
    scan_out = scan_out + skip_gain[None, :, None] * x_all.astype(jnp.float32)
    gated_out = scan_out.reshape(row_count, chan_width) * jax.nn.silu(gate_in.astype(jnp.float32))
    grouped = gated_out.reshape(row_count, local_groups, chan_width // local_groups)
    inv_rms = lax.rsqrt(jnp.mean(grouped * grouped, axis=2, keepdims=True) + 1e-05)
    normed = ((grouped * inv_rms).reshape(row_count, chan_width) * norm_gain).astype(jnp.bfloat16)
    return lax.psum_scatter(
        lax.dot_general(
            normed, w_out, (((1,), (1,)), ((), ())), preferred_element_type=jnp.float32
        ).astype(jnp.bfloat16),
        "mp",
        scatter_dimension=0,
        tiled=True,
    )


HALO = 16
MESH = pl.DeviceIdType.MESH


def remote(src, dst, send, recv, dp):
    return pltpu.make_async_remote_copy(
        src_ref=src, dst_ref=dst, send_sem=send, recv_sem=recv,
        device_id={"dp": dp}, device_id_type=MESH,
    )


def projection_kernel(
    tok_hbm, source_ref, segment_ref, w_hbm, wdt_ref,
    xb_out, dt_out, zc_out, meta_out,
    meta_ref, tokg, metas, wbuf, idxcol, onehot, packed, own,
    s_da, s_db, s_xa, s_yb, s_ya, s_xb,
    r_da, r_db, r_xa, r_yb, r_sa, r_sb,
    loc_sem, meta_send, meta_recv, w_send, w_recv,
    tok_send, tok_recv, z_send, z_recv, fwd_send, fwd_recv, red_send, red_recv,
):
    me = lax.axis_index("dp")
    core = me % 2
    chip = me // 2
    at_x = chip % 2
    at_y = chip // 2
    chip_x = chip + 1 - 2 * at_x
    chip_y = chip + 2 - 4 * at_y
    chip_d = chip_x + chip_y - chip
    sibling = me + 1 - 2 * core
    rows, depth = tok_hbm.shape[0], w_hbm.shape[0]
    width = w_hbm.shape[1] // 5
    group, state = width, width // 4
    kdim = 2 * depth
    block = 2 * rows
    na = xb_out.shape[1]
    nb = zc_out.shape[1]

    barrier = pltpu.get_barrier_semaphore()
    for k in range(1, 8):
        pl.semaphore_signal(barrier, inc=1, device_id={"dp": (me + k) % 8}, device_id_type=MESH)
    m = lax.axis_index("mp")
    beside = m + 1 - 2 * (m % 2)
    pl.semaphore_signal(barrier, inc=1, device_id={"mp": beside}, device_id_type=MESH)
    meta_ref[...] = jnp.concatenate(
        [source_ref[...], segment_ref[...], jnp.zeros((6, rows), jnp.int32)], axis=0
    )
    pl.semaphore_wait(barrier, 8)

    mine = pl.ds(pl.multiple_of(me * rows, rows), rows)

    def columns(of_chip):
        return pl.ds(pl.multiple_of(of_chip * kdim, 128), kdim)

    copies = []
    for k in range(1, 8):
        copies.append(
            remote(meta_ref, metas.at[me], meta_send.at[k - 1], meta_recv.at[k - 1], (me + k) % 8)
        )
    part = rows // 2
    half = m % 2

    def halves(dev, which):
        return pl.ds(pl.multiple_of(dev * rows + which * part, part), part)

    directs = []
    for i, to in enumerate((chip_d, chip_x, chip_y)):
        directs.append(
            remote(
                tok_hbm.at[pl.ds(pl.multiple_of(half * part, part), part), columns(to)],
                tokg.at[halves(me, half)], tok_send.at[i], tok_recv.at[i], 2 * to + core,
            )
        )
    for c in copies + directs:
        c.start()
    local = [
        pltpu.make_async_copy(tok_hbm.at[:, columns(chip)], tokg.at[mine], loc_sem.at[0]),
        pltpu.make_async_copy(meta_ref, metas.at[me], loc_sem.at[1]),
    ]
    forward = [
        remote(tok_hbm.at[:, columns(chip)], tokg.at[mine], fwd_send.at[0], fwd_recv.at[0], sibling)
    ]
    kmine = pl.ds(pl.multiple_of(core * depth, depth), depth)

    def pieces(g):
        return (
            (w_hbm.at[:, pl.ds(pl.multiple_of(g * group, 128), group)], 0, group),
            (w_hbm.at[:, pl.ds(pl.multiple_of(4 * group + g * state, 128), state)], group, state),
            (wdt_ref.at[g], na, 128),
            (w_hbm.at[:, pl.ds(pl.multiple_of(2 * group + g * group, 128), group)], na + 128, group),
            (w_hbm.at[:, pl.ds(pl.multiple_of(4 * group + 2 * state + g * state, 128), state)],
             na + 128 + group, state),
        )

    weights = []
    for i, (src, col, size) in enumerate(pieces(1 - core)):
        weights.append(
            remote(src, wbuf.at[kmine, pl.ds(col, size)], w_send.at[i], w_recv.at[i], sibling)
        )
    for i, (src, col, size) in enumerate(pieces(core)):
        local.append(
            pltpu.make_async_copy(src, wbuf.at[kmine, pl.ds(col, size)], loc_sem.at[2 + i])
        )
    for c in forward + weights + local:
        c.start()

    for c in copies:
        c.wait_recv()
    local[1].wait()
    idxcol[0:HALO, :] = jnp.full((HALO, 128), -1, jnp.int32)
    for j in range(8):
        row = metas[j, 0:1, :]
        idxcol[HALO + j * rows : HALO + (j + 1) * rows, :] = jnp.broadcast_to(row, (128, rows)).T
    meta_out[...] = metas[...]

    sources = [2 * to + core for to in (chip_d, chip_x, chip_y)]
    across = []
    for i, dev in enumerate(sources):
        directs[i].wait_recv()
        there = tokg.at[halves(dev, half)]
        across.append(
            pltpu.make_async_remote_copy(
                src_ref=there, dst_ref=there, send_sem=z_send.at[i], recv_sem=z_recv.at[i],
                device_id={"mp": beside}, device_id_type=MESH,
            )
        )
        across[i].start()
        c = remote(there, there, fwd_send.at[1 + i], fwd_recv.at[1 + i], sibling)
        c.start()
        forward.append(c)
    for i, dev in enumerate(sources):
        across[i].wait_recv()
        there = tokg.at[halves(dev, 1 - half)]
        c = remote(there, there, fwd_send.at[4 + i], fwd_recv.at[4 + i], sibling)
        c.start()
        forward.append(c)
    for c in local[:1] + local[2:]:
        c.wait()
    for c in weights + forward:
        c.wait_recv()

    lanes = lax.broadcasted_iota(jnp.int32, (block + HALO, 128), 1)

    def pack(of_chip, slot):
        ids = idxcol[pl.ds(pl.multiple_of(of_chip * block, block), block + HALO), :]

        @pl.loop(0, 8 * rows // 128)
        def _(t):
            onehot[:, pl.ds(pl.multiple_of(t * 128, 128), 128)] = jnp.where(
                ids == lanes + t * 128, 1.0, 0.0
            ).astype(jnp.bfloat16)

        @pl.loop(0, kdim // 256)
        def _(t):
            cols = pl.ds(pl.multiple_of(t * 256, 256), 256)
            packed[slot, :, cols] = jnp.dot(
                onehot[...], tokg[:, cols], preferred_element_type=jnp.float32
            ).astype(jnp.bfloat16)

    def product(slot, col, size):
        return jnp.dot(
            packed[slot], wbuf[:, pl.ds(col, size)], preferred_element_type=jnp.float32
        )

    def split(acc):
        high = acc.astype(jnp.bfloat16).astype(jnp.float32)
        return jnp.where(lanes < 16, high, acc - high).astype(jnp.bfloat16)

    def joined(ref):
        r = ref[:, na : na + 128].astype(jnp.float32)
        return r + jnp.where(lanes < 16, pltpu.roll(r, 112, 1), pltpu.roll(r, 16, 1))

    def part_a(slot, out, add=None):
        @pl.loop(0, na // 256)
        def _(t):
            col = pl.multiple_of(t * 256, 256)
            acc = product(slot, col, 256)
            if add is not None:
                acc = acc + add[:, pl.ds(col, 256)].astype(jnp.float32)
            out[:, pl.ds(col, 256)] = acc.astype(jnp.bfloat16)

        acc = product(slot, na, 128)
        if add is not None:
            acc = acc + joined(add)
        out[:, na : na + 128] = split(acc)

    def part_b(slot, out, add=None):
        @pl.loop(0, nb // 256)
        def _(t):
            col = pl.multiple_of(t * 256, 256)
            acc = product(slot, pl.multiple_of(na + 128 + col, 128), 256)
            if add is not None:
                acc = acc + add[:, pl.ds(col, 256)].astype(jnp.float32)
            out[:, pl.ds(col, 256)] = acc.astype(jnp.bfloat16)

    dev_x, dev_y = 2 * chip_x + core, 2 * chip_y + core
    c_da = remote(s_da, r_da, red_send.at[0], red_recv.at[0], dev_x)
    c_db = remote(s_db, r_db, red_send.at[1], red_recv.at[1], dev_y)
    c_xa = remote(s_xa, r_xa, red_send.at[2], red_recv.at[2], dev_x)
    c_yb = remote(s_yb, r_yb, red_send.at[3], red_recv.at[3], dev_y)
    c_ya = remote(s_ya, r_sa, red_send.at[4], red_recv.at[4], dev_y)
    c_xb = remote(s_xb, r_sb, red_send.at[5], red_recv.at[5], dev_x)
    pack(chip_d, 0)
    part_a(0, s_da)
    c_da.start()
    part_b(0, s_db)
    c_db.start()
    pack(chip_x, 1)
    part_a(1, s_xa)
    c_xa.start()
    pack(chip_y, 2)
    part_b(2, s_yb)
    c_yb.start()
    pack(chip, 0)

    @pl.loop(0, na // 256)
    def _(t):
        col = pl.multiple_of(t * 256, 256)
        own[:, pl.ds(col, 256)] = product(0, col, 256)

    own[:, na : na + 128] = product(0, na, 128)

    @pl.loop(0, nb // 256)
    def _(t):
        col = pl.multiple_of(na + 128 + t * 256, 128)
        own[:, pl.ds(col, 256)] = product(0, col, 256)

    c_da.wait_recv()
    part_a(2, s_ya, r_da)
    c_ya.start()
    c_db.wait_recv()
    part_b(1, s_xb, r_db)
    c_xb.start()
    c_xa.wait_recv()
    c_yb.wait_recv()
    c_ya.wait_recv()

    @pl.loop(0, na // 256)
    def _(t):
        cols = pl.ds(pl.multiple_of(t * 256, 256), 256)
        xb_out[:, cols] = (
            own[:, cols] + r_xa[:, cols].astype(jnp.float32) + r_sa[:, cols].astype(jnp.float32)
        ).astype(jnp.bfloat16)

    dt_out[...] = own[:, na : na + 128] + joined(r_xa) + joined(r_sa)
    c_xb.wait_recv()

    @pl.loop(0, nb // 256)
    def _(t):
        cols = pl.ds(pl.multiple_of(t * 256, 256), 256)
        own_cols = pl.ds(pl.multiple_of(na + 128 + t * 256, 128), 256)
        zc_out[:, cols] = (
            own[:, own_cols] + r_yb[:, cols].astype(jnp.float32) + r_sb[:, cols].astype(jnp.float32)
        ).astype(jnp.bfloat16)

    for c in copies + directs + across + forward + weights + [c_da, c_db, c_xa, c_yb, c_ya, c_xb]:
        c.wait_send()


def project(tokens, source, segment, w_in, wdt):
    rows, depth = tokens.shape[0], w_in.shape[0]
    width = w_in.shape[1] // 5
    na = width + width // 4
    nb = na
    m = 2 * rows + HALO
    bf = jnp.bfloat16
    vmem = pl.BlockSpec(memory_space=pltpu.VMEM)
    hbm = pl.BlockSpec(memory_space=pl.ANY)
    dma = pltpu.SemaphoreType.DMA
    a, b = pltpu.VMEM((m, na + 128), bf), pltpu.VMEM((m, nb), bf)
    return pl.pallas_call(
        projection_kernel,
        out_shape=(
            jax.ShapeDtypeStruct((m, na), bf),
            jax.ShapeDtypeStruct((m, 128), jnp.float32),
            jax.ShapeDtypeStruct((m, nb), bf),
            jax.ShapeDtypeStruct((8, 8, rows), jnp.int32),
        ),
        in_specs=[hbm, vmem, vmem, hbm, vmem],
        out_specs=(vmem,) * 4,
        scratch_shapes=[
            pltpu.VMEM((8, rows), jnp.int32),
            pltpu.VMEM((8 * rows, 2 * depth), bf),
            pltpu.VMEM((8, 8, rows), jnp.int32),
            pltpu.VMEM((2 * depth, na + 128 + nb), bf),
            pltpu.VMEM((8 * rows + HALO, 128), jnp.int32),
            pltpu.VMEM((m, 8 * rows), bf),
            pltpu.VMEM((3, m, 2 * depth), bf),
            pltpu.VMEM((m, na + 128 + nb), jnp.float32),
            a, b, a, b, a, b,
            a, b, a, b, a, b,
            dma((7,)), dma((7,)), dma((7,)), dma((5,)), dma((5,)),
            dma((3,)), dma((3,)), dma((3,)), dma((3,)), dma((7,)), dma((7,)), dma((6,)), dma((6,)),
        ],
        compiler_params=pltpu.CompilerParams(
            collective_id=0, has_side_effects=True, vmem_limit_bytes=58 << 20
        ),
    )(tokens, source, segment, w_in, wdt)


TILES = 4


def output_kernel(normed_ref, w_hbm, out_ref, whole, wbuf, own, sent, got,
                  loc_sem, sib_send, sib_recv, send_sem, recv_sem):
    dp, m = lax.axis_index("dp"), lax.axis_index("mp")
    core = dp % 2
    sibling = dp + 1 - 2 * core
    half = normed_ref.shape[0] // 2
    chans = normed_ref.shape[1]
    part = half // 4
    step = w_hbm.shape[0] // TILES

    barrier = pltpu.get_barrier_semaphore()
    pl.semaphore_signal(barrier, inc=1, device_id={"dp": sibling}, device_id_type=MESH)
    for k in range(1, 4):
        pl.semaphore_signal(barrier, inc=1, device_id={"mp": (m + k) % 4}, device_id_type=MESH)
    loads = []
    for t in range(TILES):
        rows = pl.ds(t * step, step)
        loads.append(pltpu.make_async_copy(w_hbm.at[rows], wbuf.at[rows], loc_sem.at[t]))
        loads[t].start()
    pl.semaphore_wait(barrier, 4)
    cols = pl.ds(pl.multiple_of(core * chans, chans), chans)
    swap = remote(
        normed_ref.at[pl.ds(pl.multiple_of((1 - core) * half, half), half)],
        whole.at[:, cols], sib_send, sib_recv, sibling,
    )
    swap.start()
    whole[:, cols] = normed_ref[pl.ds(pl.multiple_of(core * half, half), half), :]
    swap.wait_recv()

    inner = m * (3 - m) // 2
    end = inner * 3 * (m - 1) + (1 - inner) * m
    near = 1 + end // 3
    far = 3 - near
    opp = 3 - end

    def block(j):
        return pl.ds(pl.multiple_of(j * part, part), part)

    def hop(i, slot, to, t):
        c = pl.ds(t * step, step)
        return pltpu.make_async_remote_copy(
            src_ref=sent.at[i, :, c], dst_ref=got.at[slot, :, c],
            send_sem=send_sem.at[i, t], recv_sem=recv_sem.at[slot, t],
            device_id={"mp": to}, device_id_type=MESH,
        )

    for t in range(TILES):
        loads[t].wait()

        @pl.loop(0, step // 256)
        def _(u):
            c = pl.ds(pl.multiple_of(t * step + u * 256, 256), 256)
            own[:, c] = lax.dot_general(
                whole[...], wbuf[c, :], (((1,), (1,)), ((), ())),
                preferred_element_type=jnp.float32,
            )

        c = pl.ds(t * step, step)

        @pl.when(inner == 0)
        def _():
            for slot, j in ((2, opp), (1, far), (0, near)):
                sent[slot, :, c] = own[block(j), c].astype(jnp.bfloat16)
                hop(slot, slot, near, t).start()

        @pl.when(inner == 1)
        def _():
            sent[0, :, c] = own[block(end), c].astype(jnp.bfloat16)
            hop(0, 0, end, t).start()

    @pl.when(inner == 1)
    def _():
        for t in range(TILES):
            c = pl.ds(t * step, step)
            for i, slot, j in ((1, 1, opp), (2, 3, far)):
                held = 2 if i == 1 else 1
                hop(i, held, j, t).wait_recv()
                sent[i, :, c] = (
                    own[block(j), c] + got[held, :, c].astype(jnp.float32)
                ).astype(jnp.bfloat16)
                hop(i, slot, j, t).start()
        for t in range(TILES):
            c = pl.ds(t * step, step)
            hop(0, 0, end, t).wait_recv()
            hop(0, 3, end, t).wait_recv()
            out_ref[:, c] = (
                own[block(m), c] + got[0, :, c].astype(jnp.float32)
                + got[3, :, c].astype(jnp.float32)
            ).astype(jnp.bfloat16)

    @pl.when(inner == 0)
    def _():
        for t in range(TILES):
            c = pl.ds(t * step, step)
            hop(0, 0, near, t).wait_recv()
            hop(0, 1, near, t).wait_recv()
            out_ref[:, c] = (
                own[block(m), c] + got[0, :, c].astype(jnp.float32)
                + got[1, :, c].astype(jnp.float32)
            ).astype(jnp.bfloat16)

    for t in range(TILES):
        for i in range(3):
            hop(i, 0, near * (1 - inner) + end * inner, t).wait_send()
    swap.wait_send()


def project_out(normed, w_out):
    half, chans = normed.shape[0] // 2, normed.shape[1]
    feats = w_out.shape[0]
    bf = jnp.bfloat16
    vmem = pl.BlockSpec(memory_space=pltpu.VMEM)
    dma = pltpu.SemaphoreType.DMA
    return pl.pallas_call(
        output_kernel,
        out_shape=jax.ShapeDtypeStruct((half // 4, feats), bf),
        in_specs=[vmem, pl.BlockSpec(memory_space=pl.ANY)],
        out_specs=vmem,
        scratch_shapes=[
            pltpu.VMEM((half, 2 * chans), bf),
            pltpu.VMEM((feats, 2 * chans), bf),
            pltpu.VMEM((half, feats), jnp.float32),
            pltpu.VMEM((3, half // 4, feats), bf),
            pltpu.VMEM((4, half // 4, feats), bf),
            dma((TILES,)), dma, dma, dma((3, TILES)), dma((4, TILES)),
        ],
        compiler_params=pltpu.CompilerParams(
            collective_id=1, has_side_effects=True, vmem_limit_bytes=48 << 20
        ),
    )(normed, w_out)


def scan_kernel(
    xb_ref, dt_ref, zc_ref, metas, tapx_ref, tapbc_ref, head_ref, skip_ref, chan_ref,
    normed_ref,
    xs, bs, cs, bt, cum_t, dt_t, w_t, bias, scores, ssd, gz, entry, square, state, got, inc,
    send_sem, recv_sem,
):
    f32, bf = jnp.float32, jnp.bfloat16
    me = lax.axis_index("dp")
    core, chip = me % 2, me // 2
    block, chans = normed_ref.shape
    heads_here = chans // HEAD_DIM
    rows = block // 2
    wide = bs.shape[1]

    barrier = pltpu.get_barrier_semaphore()
    for k in range(1, 4):
        pl.semaphore_signal(
            barrier, inc=1, device_id={"dp": (me + 2 * k) % 8}, device_id_type=MESH
        )
    pl.semaphore_wait(barrier, 3)

    first, second = metas[2 * chip, 1:2, :], metas[2 * chip + 1, 1:2, :]
    earlier = metas[(2 * chip + 7) % 8, 1:2, :]
    follows = (chip + 3) // 4
    earlier = earlier * follows - (1 - follows)

    def column(row):
        return jnp.broadcast_to(row, (128, row.shape[1])).T

    seg_ext = jnp.concatenate(
        [column(earlier)[rows - HALO :], column(first), column(second)], axis=0
    )
    seg_row = jnp.concatenate([first, second], axis=1)
    seg_col = seg_ext[HALO:]
    seg_before = seg_ext[HALO - 1 : HALO]
    seg_last = seg_ext[block + HALO - 1 :]
    same = [jnp.where(pltpu.roll(seg_ext, k, 0) == seg_ext, 1.0, 0.0) for k in range(1, CONV)]

    def convolved(src, col, taps):
        v = src[:, pl.ds(col, 128)].astype(f32)
        total = taps[CONV - 1 : CONV] * v
        for k in range(1, CONV):
            total = total + same[k - 1] * (taps[CONV - 1 - k : CONV - k] * pltpu.roll(v, k, 0))
        total = total[HALO:]
        return (total / (1.0 + jnp.exp(-total))).astype(bf)

    @pl.loop(0, chans // 128)
    def _(t):
        col = pl.multiple_of(t * 128, 128)
        xs[:, pl.ds(col, 128)] = convolved(
            xb_ref, col, tapx_ref[:, pl.ds(pl.multiple_of(core * chans + col, 128), 128)]
        )

    for t in range(wide // 128):
        at = pl.ds(pl.multiple_of(core * wide + t * 128, 128), 128)
        here = pl.ds(t * 128, 128)
        bs[:, here] = convolved(xb_ref, chans + t * 128, tapbc_ref[:, 0, at])
        cs[:, here] = convolved(zc_ref, chans + t * 128, tapbc_ref[:, 1, at])
    bt[...] = bs[...].astype(f32).T.astype(bf)

    heads = head_ref[core]
    u = dt_ref[HALO:, :] + heads[0:1]
    step_dt = jnp.maximum(u, 0.0) + jnp.log1p(jnp.exp(-jnp.abs(u)))
    rate = -step_dt * heads[1:2]
    lower = jnp.where(
        lax.broadcasted_iota(jnp.int32, (block, block), 0)
        >= lax.broadcasted_iota(jnp.int32, (block, block), 1), 1.0, 0.0
    ).astype(bf)
    high = rate.astype(bf)
    middle = (rate - high.astype(f32)).astype(bf)
    low = (rate - high.astype(f32) - middle.astype(f32)).astype(bf)
    cum = (
        jnp.dot(lower, high, preferred_element_type=f32)
        + jnp.dot(lower, middle, preferred_element_type=f32)
        + jnp.dot(lower, low, preferred_element_type=f32)
    )
    cum_t[...] = cum.T
    dt_t[...] = step_dt.T
    at_last = jnp.where(seg_row == seg_row[:, block - 1 :], 1.0, 0.0)
    w_t[...] = jnp.exp(cum_t[:, block - 1 :] - cum_t[...]) * dt_t[...] * at_last
    enters = jnp.where(seg_col == seg_before, 1.0, 0.0)
    keeps = jnp.where(seg_last == seg_before, 1.0, 0.0)

    def pair_rows(ref, p):
        return ref[pl.ds(2 * p, 1), :], ref[pl.ds(2 * p + 1, 1), :]

    def pair_column(ref, p):
        a, b = pair_rows(ref, p)
        return jnp.concatenate(
            [jnp.broadcast_to(a, (64, block)), jnp.broadcast_to(b, (64, block))], axis=0
        ).T

    @pl.loop(0, chans // 128)
    def _(p):
        cols = pl.ds(pl.multiple_of(p * 128, 128), 128)
        weighted = (pair_column(w_t, p) * xs[:, cols].astype(f32)).astype(bf)
        state[0:wide, cols] = jnp.dot(
            bt[...], weighted, preferred_element_type=f32
        ).astype(bf)
        reach = jnp.exp(pair_column(cum_t, p))
        gain = jnp.broadcast_to(reach[block - 1 :] * keeps, (8, 128))
        rounded = gain.astype(bf).astype(f32)
        state[wide : wide + 16, cols] = jnp.concatenate([rounded, gain - rounded], axis=0).astype(bf)
        entry[:, cols] = reach * enters

    def leave(to):
        return remote(
            state, got.at[chip % 3], send_sem.at[to - 1], recv_sem.at[chip % 3], 2 * to + core
        )

    for to in (3, 2, 1):

        @pl.when(chip < to)
        def _():
            leave(to).start()

    scores[...] = jnp.dot(cs[...], bt[...], preferred_element_type=f32)
    for t in range(block // 128):
        here = slice(t * 128, (t + 1) * 128)
        linked = (seg_col == seg_row[:, here]) & (
            lax.broadcasted_iota(jnp.int32, (block, 128), 0)
            >= lax.broadcasted_iota(jnp.int32, (block, 128), 1) + t * 128
        )
        bias[:, here] = jnp.where(linked, 0.0, -1e30)

    lanes = lax.broadcasted_iota(jnp.int32, (rows, 128), 1)

    @pl.loop(0, chans // 128)
    def _(p):
        cols = pl.ds(pl.multiple_of(p * 128, 128), 128)
        cum_rows, dt_rows = pair_rows(cum_t, p), pair_rows(dt_t, p)
        cum_cols = [column(r) for r in cum_rows]
        for i in range(2):
            here = slice(i * rows, (i + 1) * rows)
            w = (i + 1) * rows
            outs = []
            for n in range(2):
                spans = jnp.concatenate([cum_cols[n][here]] * (w // 128), axis=1)
                spans = spans - cum_rows[n][:, :w] + bias[here, :w]
                mixing = (scores[here, :w] * jnp.exp(spans) * dt_rows[n][:, :w]).astype(bf)
                outs.append(jnp.dot(mixing, xs[0:w, cols], preferred_element_type=f32))
            skips = jnp.where(
                lanes < 64, skip_ref[core * heads_here + 2 * p], skip_ref[core * heads_here + 2 * p + 1]
            )
            ssd[here, cols] = (
                jnp.where(lanes < 64, outs[0], outs[1]) + skips * xs[here, cols].astype(f32)
            )
        z = zc_ref[:, cols].astype(f32)[HALO:]
        gz[:, cols] = z / (1.0 + jnp.exp(-z))

    inc[...] = jnp.zeros_like(inc)
    for source in range(3):

        @pl.when(source < chip)
        def _():
            remote(
                state, got.at[source], send_sem.at[0], recv_sem.at[source], (me + 2) % 8
            ).wait_recv()
            gain = (
                got[source, wide : wide + 8, :].astype(f32)
                + got[source, wide + 8 : wide + 16, :].astype(f32)
            )[0:1]
            inc[...] = gain * inc[...] + got[source, 0:wide, :].astype(f32)

    square[...] = jnp.zeros_like(square)

    @pl.loop(0, chans // 128)
    def _(p):
        cols = pl.ds(pl.multiple_of(p * 128, 128), 128)
        before = jnp.dot(cs[...], inc[:, cols].astype(bf), preferred_element_type=f32)
        gated = (ssd[:, cols] + entry[:, cols] * before) * gz[:, cols]
        ssd[:, cols] = gated
        square[...] += gated * gated

    inv = lax.rsqrt(jnp.sum(square[...], axis=1, keepdims=True) * (1.0 / chans) + 1e-05)
    inv = jnp.broadcast_to(inv, (block, 128))

    @pl.loop(0, chans // 128)
    def _(p):
        cols = pl.ds(pl.multiple_of(p * 128, 128), 128)
        at = pl.ds(pl.multiple_of(core * chans + p * 128, 128), 128)
        normed_ref[:, cols] = (ssd[:, cols] * inv * chan_ref[0:1, at]).astype(bf)

    for to in (3, 2, 1):

        @pl.when(chip < to)
        def _():
            leave(to).wait_send()


def scan(xb, dt_raw, zc, metas, conv_x, conv_bc, heads, skip, chan):
    f32, bf = jnp.float32, jnp.bfloat16
    block = xb.shape[0] - HALO
    chans = conv_x.shape[1] // 2
    wide = xb.shape[1] - chans
    dma = pltpu.SemaphoreType.DMA
    vmem = pl.BlockSpec(memory_space=pltpu.VMEM)

    def buf(shape, kind=f32):
        return pltpu.VMEM(shape, kind)

    return pl.pallas_call(
        scan_kernel,
        out_shape=jax.ShapeDtypeStruct((block, chans), bf),
        in_specs=[vmem] * 7 + [pl.BlockSpec(memory_space=pltpu.SMEM), vmem],
        out_specs=vmem,
        scratch_shapes=[
            buf((block, chans), bf), buf((block, wide), bf), buf((block, wide), bf),
            buf((wide, block), bf),
            buf((128, block)), buf((128, block)), buf((128, block)),
            buf((block, block)), buf((block, block)),
            buf((block, chans)), buf((block, chans)), buf((block, chans)), buf((block, 128)),
            buf((wide + 16, chans), bf), buf((3, wide + 16, chans), bf), buf((wide, chans)),
            dma((3,)), dma((3,)),
        ],
        compiler_params=pltpu.CompilerParams(
            collective_id=2, has_side_effects=True, vmem_limit_bytes=40 << 20
        ),
    )(xb, dt_raw, zc, metas, conv_x, conv_bc, heads, skip, chan)


def on_plane(
    tokens, pack_source, segment_ids, w_in, w_dt, w_out, conv_x, conv_bc,
    dt_bias, decay_rate, skip_gain, norm_gain,
):
    heads = w_dt.shape[1] // 2
    halves = w_dt.reshape(w_dt.shape[0], 2, heads).transpose(1, 0, 2)
    wdt = jnp.pad(jnp.concatenate([halves, halves], axis=2), ((0, 0), (0, 0), (0, 128 - 2 * heads)))
    xb, dt_raw, zc, metas = project(
        tokens, pack_source.reshape(1, -1), segment_ids.reshape(1, -1), w_in, wdt
    )
    params = jnp.stack([dt_bias, decay_rate]).reshape(2, 2, heads).transpose(1, 0, 2)
    params = jnp.pad(params, ((0, 0), (0, 6), (0, 128 - heads)))
    normed = scan(
        xb, dt_raw, zc, metas, conv_x, conv_bc, params, skip_gain, norm_gain.reshape(1, -1)
    )
    return project_out(normed, w_out)


def solution(mesh):
    placed = (
        P("dp", None),
        P("dp"),
        P("dp"),
        P("dp", "mp"),
        P("dp", "mp"),
        P(None, "mp"),
        P(None, "mp"),
        P(None, None, "mp"),
        P("mp"),
        P("mp"),
        P("mp"),
        P("mp"),
    )
    body = on_plane if mesh.shape["dp"] == 8 and mesh.shape["mp"] == 4 else on_device
    return jax.shard_map(
        body, mesh=mesh, in_specs=placed, out_specs=P(("dp", "mp"), None), check_vma=False
    )
```
